1024 devices in a mesh: seq: 8 (over x, core), dp: 128 (over z, y).
Axes of the slice: x: 4, y: 4, z: 32, core: 2. Of those that a mesh axis runs over, the one named last changes fastest.
Arguments:
- layer_input: bfloat16 [128, 2048, 4096], P('dp', None, 'seq'), may hold values from -6 to 6
- query_proj: bfloat16 [128, 2048, 512], P('dp', 'seq'), may hold values from -6 to 6
- key_proj: bfloat16 [128, 2048, 128], P('dp', 'seq'), may hold values from -6 to 6
- value_proj: bfloat16 [128, 2048, 128], P('dp', 'seq'), may hold values from -6 to 6
- out_grad: bfloat16 [128, 2048, 512], P('dp', 'seq'), may hold values from -0.1875 to 0.1875
- block_pos: int32 [128, 16], P('dp'), may hold values from 0 to 15, each once within a row
- doc_ids: int32 [128, 16], P('dp'), may hold values from 0 to 7, never falling along the last dimension, each value on 1 to 4 neighbouring positions
Outputs:
- weight_grad: float32 [4096, 768], P(('seq', 'dp'))
The draws below stay inside these ranges and needn't reach their ends.
Inputs may be any that keep to these rules, and one draw needn't show every extreme that they name: Each row is a permutation: storage block j of a sequence holds the tokens of position block block_pos[j] in order. `doc_ids`: along a row the document numbers never fall; each document covers 1 to 4 whole position blocks, and one covers exactly 4.
All inputs are finite; a program needn't handle non-finite values.
Results may differ from the reference program's by a relative error of at most 0.0062.
Values may be sent and summed in bfloat16 or wider, within the bound.
A program may use at most 32 MiB of HBM per device.

```python
import math
import jax
import jax.numpy as jnp
import numpy as np
from jax import lax

D = 4096
HD = 128
GROUP_Q = 4
BLOCK = 128
QW = 512
QKV = 768
LEN = 2048
BLOCKS = 16
SEQS = 128
DOCS = 8
MOST_DOC = 4


def draw_key_proj(key, part):
    own_key = jax.random.fold_in(key, 17)
    result = jax.random.truncated_normal(own_key, -4.0, 4.0, (SEQS, LEN, HD))
    return result.astype(jnp.bfloat16)


def draw_query_proj(key, part):
    own_key = jax.random.fold_in(key, 29)
    result = jax.random.truncated_normal(own_key, -4.0, 4.0, (SEQS, LEN, GROUP_Q, HD))
    return result.reshape(SEQS, LEN, QW).astype(jnp.bfloat16)


def shard_levels(rng, extent, cuts, low, top_value):
    def one(axis_at, blocks):
        steps = jax.random.uniform(jax.random.fold_in(jax.random.fold_in(rng, 6), axis_at), (blocks,), jnp.float32, low / len(cuts), top_value / len(cuts))
        return jnp.repeat(jnp.exp(steps), extent[axis_at] // blocks).reshape((-1,) + (1,) * (len(extent) - axis_at - 1))

    loudness = one(*cuts[0])
    for cut in cuts[1:]:
        loudness = loudness * one(*cut)
    return loudness


def split_up(count, total, bound, skew):
    weights = [(1 << 20) // math.isqrt(grade ** skew) + 1 for grade in range(2, count + 1)]
    spare, counts = total - bound - (count - 1), [1] * (count - 1)
    while spare > 0:
        free = [i for i in range(count - 1) if counts[i] < bound]
        pool, left = sum([weights[i] for i in free]), spare
        for i in free:
            addition = min(bound - counts[i], max(1, left * weights[i] // pool), spare)
            counts[i] = counts[i] + addition
            spare = spare - addition
    return np.array([bound] + counts)


def ragged(rng, count, total, limit, slope):
    if count == 2:
        one = jax.random.randint(rng, (), max(1, total - limit), min(limit, total - 1) + 1)
        return jnp.stack([one, total - one])
    tallies = jnp.asarray(split_up(count, total, limit, slope), jnp.int32)
    pairs = (count - 1) // 2
    source_of, taker = tallies[1:1 + 2 * pairs:2], tallies[2:2 + 2 * pairs:2]
    margin = jnp.minimum(source_of - 1, limit - taker)
    shifted = jax.random.randint(jax.random.fold_in(rng, 1), (pairs,), 0, 1 << 20) % (margin + 1)
    tallies = tallies.at[1:1 + 2 * pairs:2].set(source_of - shifted).at[2:2 + 2 * pairs:2].set(taker + shifted)
    return tallies[jax.random.permutation(jax.random.fold_in(rng, 2), count)]


def scatter_about(key, dims, scale, most, shards=(), held_as=jnp.bfloat16):
    level = shard_levels(key, dims, shards, -0.22, 0.18) if shards else 1.0
    values = jax.random.normal(key, dims, jnp.float32) * scale * level
    return jnp.minimum(jnp.maximum(values, -most), most).astype(held_as)


def setup_inputs(seed: int = 0) -> dict:
    streams_of = jax.random.split(jax.random.key(seed), 8)
    return {
        "layer_input": scatter_about(streams_of[0], (SEQS, LEN, D), 1.0, 6.0, ((0, 128), (2, 8))),
        "query_proj": draw_query_proj(jax.random.fold_in(streams_of[7], 71), 0),
        "key_proj": draw_key_proj(jax.random.fold_in(streams_of[7], 71), 0),
        "value_proj": scatter_about(streams_of[3], (SEQS, LEN, HD), 1.0, 6.0, ((0, 128), (1, 8))),
        "out_grad": scatter_about(streams_of[4], (SEQS, LEN, QW), (16 * (LEN * SEQS) ** -0.5), 0.1875, ((0, 128), (1, 8))),
        "block_pos": jax.vmap(lambda own: jax.random.permutation(own, BLOCKS))(jax.random.split(streams_of[5], SEQS)).reshape((SEQS, BLOCKS)).astype(jnp.int32),
        "doc_ids": jax.vmap(lambda own: jnp.searchsorted(jnp.cumsum(ragged(own, DOCS, BLOCKS, MOST_DOC, 1)), jnp.arange(BLOCKS), side="right"))(jax.random.split(streams_of[6], SEQS)).reshape((SEQS, BLOCKS)).astype(jnp.int32),
    }


def one_sequence(query_s, key_s, value_s, grad_s, pos_row, doc_row):
    precise = lax.Precision.HIGHEST
    row_index = jnp.arange(LEN, dtype=jnp.int32)
    block_at = pos_row[row_index // BLOCK]
    token_pos = block_at * BLOCK + row_index % BLOCK
    token_doc = doc_row[block_at]
    live_mask = (token_doc[:, None] == token_doc[None, :]) & (token_pos[:, None] >= token_pos[None, :])
    scaling = HD ** -0.5
    queries = query_s.astype(jnp.float32).reshape(LEN, GROUP_Q, HD)
    key_rows = key_s.astype(jnp.float32)
    value_rows = value_s.astype(jnp.float32)
    grad_heads = grad_s.astype(jnp.float32).reshape(LEN, GROUP_Q, HD)
    scores = jnp.einsum("ihc,jc->hij", queries, key_rows, precision=precise) * scaling
    masked = jnp.where(live_mask[None], scores, -1e30)
    row_peak = jnp.max(masked, axis=2, keepdims=True)
    weights_exp = jnp.where(live_mask[None], jnp.exp(masked - row_peak), 0.0)
    probs = weights_exp / jnp.sum(weights_exp, axis=2, keepdims=True)
    probs_b = lax.optimization_barrier(probs.astype(jnp.bfloat16)).astype(jnp.float32)
    attended = jnp.einsum("hij,jc->hic", probs_b, value_rows, precision=precise)
    row_delta = jnp.sum(jnp.transpose(grad_heads, (1, 0, 2)) * attended, axis=2)
    dprobs = jnp.einsum("ihc,jc->hij", grad_heads, value_rows, precision=precise)
    dscores = probs * (dprobs - row_delta[..., None])
    dscores = lax.optimization_barrier(dscores.astype(jnp.bfloat16)).astype(jnp.float32)
    query_grad = jnp.einsum("hij,jc->ihc", dscores, key_rows, precision=precise) * scaling
    query_grad = query_grad.reshape(LEN, QW).astype(jnp.bfloat16)
    key_grad = (jnp.einsum("hij,ihc->jc", dscores, queries, precision=precise) * scaling).astype(jnp.bfloat16)
    value_grad = jnp.einsum("hij,ihc->jc", probs_b, grad_heads, precision=precise).astype(jnp.bfloat16)
    return jnp.concatenate([query_grad, key_grad, value_grad], axis=1)


def reference(layer_input, query_proj, key_proj, value_proj, out_grad, block_pos, doc_ids):
    def advance(accum, seq_items):
        input_s, query_s, key_s, value_s, grad_s, pos_row, doc_row = seq_items
        grad_rows = one_sequence(query_s, key_s, value_s, grad_s, pos_row, doc_row)
        weight_term = lax.dot_general(input_s, grad_rows, (((0,), (0,)), ((), ())), preferred_element_type=jnp.float32)
        return accum + weight_term, None

    start_value = jnp.zeros((D, QKV), jnp.float32)
    accum, _ = lax.scan(advance, start_value, (layer_input, query_proj, key_proj, value_proj, out_grad, block_pos, doc_ids))
    return accum
```

```python
import functools

import jax
import jax.numpy as jnp
from jax import lax
from jax.experimental import pallas as pl
from jax.experimental.pallas import tpu as pltpu
from jax.sharding import PartitionSpec as P

MESH = pl.DeviceIdType.MESH
F32 = jnp.float32
BF16 = jnp.bfloat16
FILL = -1e30
BLK = 128
HD = 128
NT = (((1,), (1,)), ((), ()))
NN = (((1,), (0,)), ((), ()))
TN = (((0,), (0,)), ((), ()))


def dot(a, b, dims):
    return lax.dot_general(a, b, dims, preferred_element_type=F32)


class Links:
    def __init__(self, send_sems, recv_sems):
        self.send_sems, self.recv_sems = send_sems, recv_sems
        self.count = 0
        self.sent = []

    def copy(self, src, dst, device):
        made = pltpu.make_async_remote_copy(
            src_ref=src,
            dst_ref=dst,
            send_sem=self.send_sems.at[self.count],
            recv_sem=self.recv_sems.at[self.count],
            device_id=device,
            device_id_type=MESH,
        )
        self.count += 1
        self.sent.append(made)
        return made


class Gather:
    def __init__(self, links, buf, ring):
        self.buf = buf
        here, left, right, far, dev_left, dev_right, dev_pair = ring
        cp = links.copy
        self.c = [
            cp(buf.at[here], buf.at[here], dev_right),
            cp(buf.at[here], buf.at[here], dev_left),
            cp(buf.at[here], buf.at[here], dev_pair),
            cp(buf.at[left, 0], buf.at[left, 0], dev_right),
            cp(buf.at[right, 1], buf.at[right, 1], dev_left),
            cp(buf.at[left], buf.at[left], dev_pair),
            cp(buf.at[right], buf.at[right], dev_pair),
            cp(buf.at[far, 0], buf.at[far, 0], dev_pair),
            cp(buf.at[far, 1], buf.at[far, 1], dev_pair),
        ]

    def begin(self):
        for k in (0, 1, 2):
            self.c[k].start()

    def relay(self):
        self.c[0].wait_recv()
        self.c[3].start()
        self.c[5].start()
        self.c[1].wait_recv()
        self.c[4].start()
        self.c[6].start()

    def last(self):
        self.c[3].wait_recv()
        self.c[7].start()
        self.c[4].wait_recv()
        self.c[8].start()

    def end(self):
        for k in (2, 5, 6, 7, 8):
            self.c[k].wait_recv()


class RingSum:
    def __init__(self, links, out, via, got, place, dev_left, dev_right):
        self.out, self.via, self.got = out, via, got
        self.place = place
        self.left, self.right = lax.rem(place + 3, 4), lax.rem(place + 1, 4)
        far = lax.rem(place + 2, 4)
        cp = links.copy
        self.c = [
            cp(out.at[far, 0], via.at[0], dev_right),
            cp(out.at[far, 1], via.at[1], dev_left),
            cp(out.at[self.right, 1], got.at[0, 1], dev_right),
            cp(out.at[self.left, 0], got.at[1, 0], dev_left),
            cp(out.at[self.right, 0], got.at[0, 0], dev_right),
            cp(out.at[self.left, 1], got.at[1, 1], dev_left),
        ]

    def begin(self):
        for k in range(4):
            self.c[k].start()

    def relay(self):
        for k, there in ((0, self.right), (1, self.left)):
            self.c[k].wait_recv()
            both = self.out[there, k].astype(F32) + self.via[k].astype(F32)
            self.out[there, k] = both.astype(BF16)
            self.c[4 + k].start()

    def end(self):
        for k in (2, 3, 4, 5):
            self.c[k].wait_recv()

    def arrived(self, half):
        return self.got[0, half].astype(F32) + self.got[1, half].astype(F32)


class LineSum:
    def __init__(self, links, out, got, place, device_of):
        self.got = got
        self.c = []
        for k in (1, 2, 3):
            there = lax.rem(place + k, 4)
            self.c.append(links.copy(out.at[there], got.at[k - 1], device_of(there)))

    def begin(self):
        for c in self.c:
            c.start()

    def end(self):
        for c in self.c:
            c.wait_recv()

    def arrived(self):
        return self.got[0].astype(F32) + self.got[1].astype(F32) + self.got[2].astype(F32)


def kernel(
    pos_ref, doc_ref, x_hbm, q_hbm, k_hbm, v_hbm, og_hbm, out_ref,
    kv, q_v, og_v, x_v, xt, g_q, g_kv, key_at, bias_at, slot_at,
    part, pair_out, pair_got, keep, sx_out, sx_via, sx_got,
    yq_out, yq_via, yq_got, yk_out, yk_via, yk_got,
    zq_own, zq_out, zq_got, zk_own, zk_out, zk_got,
    rows, piece, fwd_out, fwd_got, bwd_out, bwd_got,
    local_sems, send_sems, recv_sems,
):
    me, dp = lax.axis_index("seq"), lax.axis_index("dp")
    x, c = me // 2, me % 2
    z, y = dp // 4, dp % 4
    zh, zl = z // 4, z % 4

    def at_x(place, core):
        return lax.rem(place, 4) * 2 + core

    left, right, far, pair = at_x(x + 3, c), at_x(x + 1, c), at_x(x + 2, c), at_x(x, 1 - c)
    y_left = (me, z * 4 + lax.rem(y + 3, 4))
    y_right = (me, z * 4 + lax.rem(y + 1, 4))

    def near(place):
        return (me, (zh * 4 + place) * 4 + y)

    def group(place):
        return (me, (lax.rem(place, 8) * 4 + zl) * 4 + y)

    z_prev, z_next = group(zh + 7), group(zh + 1)

    loads = [
        pltpu.make_async_copy(k_hbm, kv.at[me, :, :, pl.ds(0, HD)], local_sems.at[0]),
        pltpu.make_async_copy(v_hbm, kv.at[me, :, :, pl.ds(HD, HD)], local_sems.at[1]),
        pltpu.make_async_copy(x_hbm, x_v, local_sems.at[2]),
        pltpu.make_async_copy(q_hbm, q_v, local_sems.at[3]),
        pltpu.make_async_copy(og_hbm, og_v, local_sems.at[4]),
    ]
    for load in loads:
        load.start()

    barrier = pltpu.get_barrier_semaphore()
    peers = [(left, dp), (right, dp), (pair, dp), y_left, y_right, z_prev, z_next]
    peers += [near(lax.rem(zl + k, 4)) for k in (1, 2, 3)]
    for peer in peers:
        pl.semaphore_signal(barrier, inc=1, device_id=peer, device_id_type=MESH)
    pl.semaphore_wait(barrier, len(peers))

    links = Links(send_sems, recv_sems)
    ring = (me, left, right, far, (left, dp), (right, dp), (pair, dp))
    gather_kv = Gather(links, kv, ring)
    loads[0].wait()
    loads[1].wait()
    gather_kv.begin()

    hits = []
    for q in range(2):
        mine = pos_ref[0, me * 2 + q]
        doc = doc_ref[0, mine]
        key_at[q * 4] = me * 2 + q
        bias_at[q * 4] = jnp.float32(0.0)
        for j in range(1, 4):
            want = jnp.maximum(mine - j, 0)
            live = jnp.logical_and(mine >= j, doc_ref[0, want] == doc)
            spot = jnp.int32(0)
            for s in range(16):
                spot = jnp.where(pos_ref[0, s] == want, jnp.int32(s), spot)
            key_at[q * 4 + j] = spot
            bias_at[q * 4 + j] = jnp.where(live, jnp.float32(0.0), jnp.float32(FILL))
            hits.append((q, q * 4 + j, jnp.where(live, spot, jnp.int32(-1))))
    for s in range(16):
        for q in range(2):
            slot = jnp.int32(8)
            for owner, number, spot in hits:
                if owner == q:
                    slot = jnp.where(spot == s, jnp.int32(number), slot)
            slot_at[q * 16 + s] = slot

    loads[2].wait()
    new = lax.broadcasted_iota(jnp.int32, (512, 512), 0)
    old = lax.broadcasted_iota(jnp.int32, (512, 512), 1)
    source = (new // 4 % 8) * 64 + (new // 32 % 4) * 16 + (new // 128) * 4 + new % 4
    one_hot = (old == source).astype(F32).astype(BF16)

    def flip(t, carry):
        at = pl.multiple_of(t * 256, 256)
        xt[:, pl.ds(at, 256)] = dot(one_hot, x_v[pl.ds(at, 256), :], NT).astype(BF16)
        return carry

    lax.fori_loop(0, 4, flip, 0)
    gather_kv.relay()
    lax.fori_loop(4, 8, flip, 0)
    gather_kv.last()
    part[...] = jnp.zeros_like(part)
    loads[3].wait()
    loads[4].wait()
    gather_kv.end()

    scaling = HD ** (-0.5)
    key_row = lax.broadcasted_iota(jnp.int32, (BLK, 2 * BLK), 0)
    query_col = lax.broadcasted_iota(jnp.int32, (BLK, 2 * BLK), 1) % BLK
    causal = key_row <= query_col

    def attend(step, carry):
        q, pair_of_heads = step // 2, step % 2
        cols = pl.ds(pl.multiple_of(pair_of_heads * 256, 256), 256)
        q_two, og_two = q_v[q, :, cols], og_v[q, :, cols]
        queries = jnp.concatenate([q_two[:, :HD], q_two[:, HD:]], axis=0)
        grads = jnp.concatenate([og_two[:, :HD], og_two[:, HD:]], axis=0)
        blocks = []
        for j in range(4):
            spot = key_at[q * 4 + j]
            blocks.append(kv[spot // 2, spot % 2])
        both = jnp.concatenate(blocks, axis=0)
        keys, values = both[:, :HD], both[:, HD:]
        scores = dot(keys, queries, NT) * scaling
        masked = [jnp.where(causal, scores[:BLK], FILL)]
        for j in range(1, 4):
            masked.append(scores[j * BLK : (j + 1) * BLK] + bias_at[q * 4 + j])
        scores = jnp.concatenate(masked, axis=0)
        peak = jnp.max(scores, axis=0, keepdims=True)
        weights = jnp.exp(scores - peak)
        probs = weights * (1.0 / jnp.sum(weights, axis=0, keepdims=True))
        probs_b = probs.astype(BF16)
        dprobs = dot(values, grads, NT)
        delta = jnp.sum(probs_b.astype(F32) * dprobs, axis=0, keepdims=True)
        dscores = (probs * (dprobs - delta)).astype(BF16)
        dq = (dot(dscores, keys, TN) * scaling).astype(BF16)
        g_q[me, q, :, cols] = jnp.concatenate([dq[:BLK], dq[BLK:]], axis=1)
        dk = dot(dscores, queries, NN) * scaling
        dv = dot(probs_b, grads, NN)
        for j in range(4):
            block = slice(j * BLK, (j + 1) * BLK)
            part[q * 4 + j, :, :HD] += dk[block]
            part[q * 4 + j, :, HD:] += dv[block]
        return carry

    lax.fori_loop(0, 4, attend, 0)

    def to_block(core, half, place):
        s = (place * 2 + core) * 2 + half
        return part[slot_at[s]] + part[slot_at[16 + s]]

    def for_pair(place, carry):
        for half in range(2):
            pair_out[place, half] = to_block(1 - c, half, place).astype(BF16)
        return carry

    lax.fori_loop(0, 4, for_pair, 0)
    gather_q = Gather(links, g_q, ring)
    gather_q.begin()
    pair_copy = links.copy(pair_out, pair_got, (pair, dp))
    pair_copy.start()

    def for_self(place, carry):
        for half in range(2):
            keep[place, half] = to_block(c, half, place)
        return carry

    lax.fori_loop(0, 4, for_self, 0)
    sum_x = RingSum(links, sx_out, sx_via, sx_got, x, (left, dp), (right, dp))
    pair_copy.wait_recv()

    def join(place, carry):
        for half in range(2):
            total = keep[place, half] + pair_got[place, half].astype(F32)
            keep[place, half] = total
            sx_out[place, half] = total.astype(BF16)
        return carry

    lax.fori_loop(0, 4, join, 0)
    sum_x.begin()
    gather_q.relay()
    sum_x.relay()
    gather_q.last()
    sum_x.end()
    for half in range(2):
        total = part[half * 4] + keep[x, half] + sum_x.arrived(half)
        g_kv[me, half] = total.astype(BF16)
    gather_g = Gather(links, g_kv, ring)
    gather_g.begin()
    gather_q.end()

    def weigh(g_ref, out, columns):
        def tile(t, carry):
            cols = pl.ds(pl.multiple_of(t * 256, 256), 256)
            grads = g_ref[:, :, :, cols].reshape(2048, 256)
            term = dot(xt[...], grads, NN).astype(BF16)
            for k in range(4):
                for half in range(2):
                    out[k, half, :, cols] = term[k * 128 + half * 64 : k * 128 + half * 64 + 64]
            return carry

        lax.fori_loop(0, columns // 256, tile, 0)

    weigh(g_q, yq_out, 512)
    sum_yq = RingSum(links, yq_out, yq_via, yq_got, y, y_left, y_right)
    sum_yq.begin()
    gather_g.relay()
    gather_g.last()
    sum_yq.relay()
    gather_g.end()
    weigh(g_kv, yk_out, 256)
    sum_yk = RingSum(links, yk_out, yk_via, yk_got, y, y_left, y_right)
    sum_yk.begin()

    def to_line(sums, own, out):
        for half in range(2):
            total = sums.out[y, half].astype(F32) + sums.arrived(half)
            for k in range(2):
                some = total[k * 32 : (k + 1) * 32]
                own[half * 2 + k] = some
                out[half * 2 + k] = some.astype(BF16)

    sum_yq.end()
    to_line(sum_yq, zq_own, zq_out)
    line_q = LineSum(links, zq_out, zq_got, zl, near)
    line_q.begin()
    sum_yk.relay()
    sum_yk.end()
    to_line(sum_yk, zk_own, zk_out)
    line_k = LineSum(links, zk_out, zk_got, zl, near)
    line_k.begin()
    line_q.end()
    rows[:, :512] = zq_own[zl] + line_q.arrived()
    line_k.end()
    rows[:, 512:] = zk_own[zl] + line_k.arrived()
    for k in range(8):
        piece[k] = rows[k * 4 : (k + 1) * 4, :]

    fwd = [links.copy(fwd_out.at[k], fwd_got.at[k], z_next) for k in range(4)]
    bwd = [links.copy(bwd_out.at[k], bwd_got.at[k], z_prev) for k in range(3)]
    for k in range(4):
        ahead = piece[lax.rem(zh + 4 - k, 8)]
        if k > 0:
            fwd[k - 1].wait_recv()
            ahead = ahead + fwd_got[k - 1]
        fwd_out[k] = ahead
        fwd[k].start()
        if k < 3:
            behind = piece[lax.rem(zh + 5 + k, 8)]
            if k > 0:
                bwd[k - 1].wait_recv()
                behind = behind + bwd_got[k - 1]
            bwd_out[k] = behind
            bwd[k].start()
    bwd[2].wait_recv()
    near_sum = piece[zh] + bwd_got[2]
    fwd[3].wait_recv()
    out_ref[...] = near_sum + fwd_got[3]
    for made in links.sent:
        made.wait_send()


def body(layer_input, query_proj, key_proj, value_proj, out_grad, block_pos, doc_ids):
    hbm = pl.BlockSpec(memory_space=pl.ANY)
    smem = pl.BlockSpec(memory_space=pltpu.SMEM)

    def ring_buffers(half_rows, columns):
        return [
            pltpu.VMEM((4, 2, half_rows, columns), BF16),
            pltpu.VMEM((2, half_rows, columns), BF16),
            pltpu.VMEM((2, 2, half_rows, columns), BF16),
        ]

    def line_buffers(columns):
        return [
            pltpu.VMEM((4, 32, columns), F32),
            pltpu.VMEM((4, 32, columns), BF16),
            pltpu.VMEM((3, 32, columns), BF16),
        ]

    copies = 3 * 9 + 1 + 3 * 6 + 2 * 3 + 7
    return pl.pallas_call(
        kernel,
        out_shape=jax.ShapeDtypeStruct((4, 768), F32),
        in_specs=[smem, smem, hbm, hbm, hbm, hbm, hbm],
        out_specs=pl.BlockSpec(memory_space=pltpu.VMEM),
        scratch_shapes=[
            pltpu.VMEM((8, 2, BLK, 256), BF16),
            pltpu.VMEM((2, BLK, 512), BF16),
            pltpu.VMEM((2, BLK, 512), BF16),
            pltpu.VMEM((2048, 512), BF16),
            pltpu.VMEM((512, 2048), BF16),
            pltpu.VMEM((8, 2, BLK, 512), BF16),
            pltpu.VMEM((8, 2, BLK, 256), BF16),
            pltpu.SMEM((8,), jnp.int32),
            pltpu.SMEM((8,), F32),
            pltpu.SMEM((32,), jnp.int32),
            pltpu.VMEM((9, BLK, 256), F32),
            pltpu.VMEM((4, 2, BLK, 256), BF16),
            pltpu.VMEM((4, 2, BLK, 256), BF16),
            pltpu.VMEM((4, 2, BLK, 256), F32),
            *ring_buffers(BLK, 256),
            *ring_buffers(64, 512),
            *ring_buffers(64, 256),
            *line_buffers(512),
            *line_buffers(256),
            pltpu.VMEM((32, 768), F32),
            pltpu.VMEM((8, 4, 768), F32),
            pltpu.VMEM((4, 4, 768), F32),
            pltpu.VMEM((4, 4, 768), F32),
            pltpu.VMEM((3, 4, 768), F32),
            pltpu.VMEM((3, 4, 768), F32),
            pltpu.SemaphoreType.DMA((5,)),
            pltpu.SemaphoreType.DMA((copies,)),
            pltpu.SemaphoreType.DMA((copies,)),
        ],
        compiler_params=pltpu.CompilerParams(
            collective_id=0, has_side_effects=True, vmem_limit_bytes=56 * 1024 * 1024
        ),
    )(
        block_pos,
        doc_ids,
        layer_input.reshape(2048, 512),
        query_proj.reshape(2, BLK, 512),
        key_proj.reshape(2, BLK, HD),
        value_proj.reshape(2, BLK, HD),
        out_grad.reshape(2, BLK, 512),
    )


def solution(mesh):
    placed = (
        P("dp", None, "seq"),
        P("dp", "seq", None),
        P("dp", "seq", None),
        P("dp", "seq", None),
        P("dp", "seq", None),
        P("dp", None),
        P("dp", None),
    )
    return jax.shard_map(
        body, mesh=mesh, in_specs=placed, out_specs=P(("seq", "dp"), None), check_vma=False
    )
```

```python
import functools

import jax
import jax.numpy as jnp
from jax import lax
from jax.experimental import pallas as pl
from jax.experimental.pallas import tpu as pltpu
from jax.sharding import PartitionSpec as P

MESH = pl.DeviceIdType.MESH
F32 = jnp.float32
BF16 = jnp.bfloat16
FILL = -1e30
BLK = 128
HD = 128
COPIES = 4 * 11 + 1 + 3 * 6 + 2 * 3 + 2 * 7
NT = (((1,), (1,)), ((), ()))
NN = (((1,), (0,)), ((), ()))
TN = (((0,), (0,)), ((), ()))


def dot(a, b, dims):
    return lax.dot_general(a, b, dims, preferred_element_type=F32)


class Links:
    def __init__(self, send_sems, recv_sems):
        self.send_sems, self.recv_sems = send_sems, recv_sems
        self.count = 0
        self.sent = []

    def copy(self, src, dst, device):
        made = pltpu.make_async_remote_copy(
            src_ref=src,
            dst_ref=dst,
            send_sem=self.send_sems.at[self.count],
            recv_sem=self.recv_sems.at[self.count],
            device_id=device,
            device_id_type=MESH,
        )
        self.count += 1
        self.sent.append(made)
        return made


class Gather:
    def __init__(self, links, whole, half, ring):
        here, left, right, far, dev_left, dev_right, dev_pair = ring
        plan = [
            (half(here, 0), dev_right),
            (half(here, 1), dev_left),
            (half(here, 1), dev_right),
            (half(here, 0), dev_left),
            (whole(here), dev_pair),
            (half(left, 0), dev_right),
            (half(right, 1), dev_left),
            (whole(left), dev_pair),
            (whole(right), dev_pair),
            (half(far, 0), dev_pair),
            (half(far, 1), dev_pair),
        ]
        self.c = [links.copy(ref, ref, device) for ref, device in plan]

    def begin(self):
        for k in range(5):
            self.c[k].start()

    def forward(self, arrives, leaves):
        for k, m in zip(arrives, leaves):
            self.c[k].wait_recv()
            self.c[m].start()

    def relay(self):
        self.forward((0, 1), (5, 6))

    def share(self):
        self.forward((2, 3), (7, 8))

    def last(self):
        self.forward((5, 6), (9, 10))

    def end(self):
        for k in (4, 7, 8, 9, 10):
            self.c[k].wait_recv()


class RingSum:
    def __init__(self, links, out, via, got, place, dev_left, dev_right):
        self.out, self.via, self.got = out, via, got
        self.place = place
        self.left, self.right = lax.rem(place + 3, 4), lax.rem(place + 1, 4)
        far = lax.rem(place + 2, 4)
        cp = links.copy
        self.c = [
            cp(out.at[far, 0], via.at[0], dev_right),
            cp(out.at[far, 1], via.at[1], dev_left),
            cp(out.at[self.right, 1], got.at[0, 1], dev_right),
            cp(out.at[self.left, 0], got.at[1, 0], dev_left),
            cp(out.at[self.right, 0], got.at[0, 0], dev_right),
            cp(out.at[self.left, 1], got.at[1, 1], dev_left),
        ]

    def begin(self):
        for k in range(4):
            self.c[k].start()

    def relay(self):
        for k, there in ((0, self.right), (1, self.left)):
            self.c[k].wait_recv()
            both = self.out[there, k].astype(F32) + self.via[k].astype(F32)
            self.out[there, k] = both.astype(BF16)
            self.c[4 + k].start()

    def end(self):
        for k in (2, 3, 4, 5):
            self.c[k].wait_recv()

    def arrived(self, half):
        return self.got[0, half].astype(F32) + self.got[1, half].astype(F32)


class LineSum:
    def __init__(self, links, out, got, place, device_of):
        self.got = got
        self.c = []
        for k in (1, 2, 3):
            there = lax.rem(place + k, 4)
            self.c.append(links.copy(out.at[there], got.at[k - 1], device_of(there)))

    def begin(self):
        for c in self.c:
            c.start()

    def end(self):
        for c in self.c:
            c.wait_recv()

    def arrived(self):
        return self.got[0].astype(F32) + self.got[1].astype(F32) + self.got[2].astype(F32)


def kernel(
    pos_hbm, doc_hbm, x_hbm, q_hbm, k_hbm, v_hbm, og_hbm, out_ref,
    pos_ref, doc_ref, kv, q_v, og_v, x_v, xt, g_q, g_kv, key_at, bias_at, slot_at,
    part, pair_out, pair_got, keep, sx_out, sx_via, sx_got,
    yq_out, yq_via, yq_got, yk_out, yk_via, yk_got,
    zq_own, zq_out, zq_got, zk_own, zk_out, zk_got,
    fq_own, fq_out, fq_got, fk_own, fk_out, fk_got,
    local_sems, known_sems, send_sems, recv_sems,
):
    me, dp = lax.axis_index("seq"), lax.axis_index("dp")
    x, c = me // 2, me % 2
    z, y = dp // 4, dp % 4
    zh, zl = z // 4, z % 4

    def at_x(place, core):
        return lax.rem(place, 4) * 2 + core

    left, right, far, pair = at_x(x + 3, c), at_x(x + 1, c), at_x(x + 2, c), at_x(x, 1 - c)
    y_left = (me, z * 4 + lax.rem(y + 3, 4))
    y_right = (me, z * 4 + lax.rem(y + 1, 4))

    def near(place):
        return (me, (zh * 4 + place) * 4 + y)

    def group(place):
        return (me, (lax.rem(place, 8) * 4 + zl) * 4 + y)

    def at_z(shift):
        return (me, lax.rem(z + shift + 32, 32) * 4 + y)

    loads = [
        pltpu.make_async_copy(k_hbm, kv.at[me, :, :, pl.ds(0, HD)], local_sems.at[0]),
        pltpu.make_async_copy(v_hbm, kv.at[me, :, :, pl.ds(HD, HD)], local_sems.at[1]),
        pltpu.make_async_copy(x_hbm, x_v, local_sems.at[2]),
        pltpu.make_async_copy(q_hbm, q_v, local_sems.at[3]),
        pltpu.make_async_copy(og_hbm, og_v, local_sems.at[4]),
        pltpu.make_async_copy(pos_hbm, pos_ref, local_sems.at[5]),
        pltpu.make_async_copy(doc_hbm, doc_ref, local_sems.at[6]),
    ]
    for load in loads:
        load.start()

    barrier = pltpu.get_barrier_semaphore()
    peers = [(left, dp), (right, dp), (pair, dp), y_left, y_right, at_z(-1), at_z(1)]
    for peer in peers:
        pl.semaphore_signal(barrier, inc=1, device_id=peer, device_id_type=MESH)
    pl.semaphore_wait(barrier, len(peers))

    links = Links(send_sems, recv_sems)
    ring = (me, left, right, far, (left, dp), (right, dp), (pair, dp))
    gather_kv = Gather(links, lambda d: kv.at[d], lambda d, h: kv.at[d, h], ring)
    loads[0].wait()
    loads[1].wait()
    gather_kv.begin()

    def tell(r):
        for side, way in enumerate((1, -1)):
            pl.semaphore_signal(
                known_sems.at[2 * r + side], inc=1, device_id=at_z(way * 2**r), device_id_type=MESH
            )

    def hear(r):
        for side in range(2):
            pl.semaphore_wait(known_sems.at[2 * r + side], 1)

    tell(0)
    loads[5].wait()
    loads[6].wait()

    hits = []
    for q in range(2):
        mine = pos_ref[0, me * 2 + q]
        doc = doc_ref[0, mine]
        key_at[q * 4] = me * 2 + q
        bias_at[q * 4] = jnp.float32(0.0)
        for j in range(1, 4):
            want = jnp.maximum(mine - j, 0)
            live = jnp.logical_and(mine >= j, doc_ref[0, want] == doc)
            spot = jnp.int32(0)
            for s in range(16):
                spot = jnp.where(pos_ref[0, s] == want, jnp.int32(s), spot)
            key_at[q * 4 + j] = spot
            bias_at[q * 4 + j] = jnp.where(live, jnp.float32(0.0), jnp.float32(FILL))
            hits.append((q, q * 4 + j, jnp.where(live, spot, jnp.int32(-1))))
    for s in range(16):
        for q in range(2):
            slot = jnp.int32(8)
            for owner, number, spot in hits:
                if owner == q:
                    slot = jnp.where(spot == s, jnp.int32(number), slot)
            slot_at[q * 16 + s] = slot

    loads[2].wait()
    new = lax.broadcasted_iota(jnp.int32, (512, 512), 0)
    old = lax.broadcasted_iota(jnp.int32, (512, 512), 1)
    source = (new // 4 % 8) * 64 + (new // 32 % 4) * 16 + (new // 128) * 4 + new % 4
    one_hot = (old == source).astype(F32).astype(BF16)

    def flip(t, carry):
        at = pl.multiple_of(t * 256, 256)
        xt[:, pl.ds(at, 256)] = dot(one_hot, x_v[pl.ds(at, 256), :], NT).astype(BF16)
        return carry

    lax.fori_loop(0, 4, flip, 0)
    gather_kv.relay()
    hear(0)
    tell(1)
    gather_kv.share()
    lax.fori_loop(4, 8, flip, 0)
    gather_kv.last()
    part[...] = jnp.zeros_like(part)
    loads[3].wait()
    loads[4].wait()
    hear(1)
    tell(2)
    gather_kv.end()

    scaling = HD ** (-0.5)
    key_row = lax.broadcasted_iota(jnp.int32, (BLK, 2 * BLK), 0)
    query_col = lax.broadcasted_iota(jnp.int32, (BLK, 2 * BLK), 1) % BLK
    causal = key_row <= query_col

    def attend(step, carry):
        q, pair_of_heads = step // 2, step % 2
        cols = pl.ds(pl.multiple_of(pair_of_heads * 256, 256), 256)
        q_two, og_two = q_v[q, :, cols], og_v[q, :, cols]
        queries = jnp.concatenate([q_two[:, :HD], q_two[:, HD:]], axis=0)
        grads = jnp.concatenate([og_two[:, :HD], og_two[:, HD:]], axis=0)
        blocks = []
        for j in range(4):
            spot = key_at[q * 4 + j]
            blocks.append(kv[spot // 2, spot % 2])
        both = jnp.concatenate(blocks, axis=0)
        keys, values = both[:, :HD], both[:, HD:]
        scores = dot(keys, queries, NT) * scaling
        masked = [jnp.where(causal, scores[:BLK], FILL)]
        for j in range(1, 4):
            masked.append(scores[j * BLK : (j + 1) * BLK] + bias_at[q * 4 + j])
        scores = jnp.concatenate(masked, axis=0)
        peak = jnp.max(scores, axis=0, keepdims=True)
        weights = jnp.exp(scores - peak)
        probs = weights * (1.0 / jnp.sum(weights, axis=0, keepdims=True))
        probs_b = probs.astype(BF16)
        dprobs = dot(values, grads, NT)
        delta = jnp.sum(probs_b.astype(F32) * dprobs, axis=0, keepdims=True)
        dscores = (probs * (dprobs - delta)).astype(BF16)
        dq = (dot(dscores, keys, TN) * scaling).astype(BF16)
        g_q[me, q, :, cols] = jnp.concatenate([dq[:BLK], dq[BLK:]], axis=1)
        dk = dot(dscores, queries, NN) * scaling
        dv = dot(probs_b, grads, NN)
        for j in range(4):
            block = slice(j * BLK, (j + 1) * BLK)
            part[q * 4 + j, :, :HD] += dk[block]
            part[q * 4 + j, :, HD:] += dv[block]
        return carry

    def gather_queries(q):
        def half(d, h):
            return g_q.at[d, q, pl.ds(h * 64, 64)]

        return Gather(links, lambda d: g_q.at[d, q], half, ring)

    gather_a, gather_b = gather_queries(0), gather_queries(1)
    lax.fori_loop(0, 2, attend, 0)
    gather_a.begin()
    lax.fori_loop(2, 4, attend, 0)

    def to_block(core, half, place):
        s = (place * 2 + core) * 2 + half
        return part[slot_at[s]] + part[slot_at[16 + s]]

    def for_pair(place, carry):
        for half in range(2):
            pair_out[place, half] = to_block(1 - c, half, place).astype(BF16)
        return carry

    lax.fori_loop(0, 4, for_pair, 0)
    pair_copy = links.copy(pair_out, pair_got, (pair, dp))
    pair_copy.start()

    def for_self(place, carry):
        for half in range(2):
            keep[place, half] = to_block(c, half, place)
        return carry

    lax.fori_loop(0, 4, for_self, 0)
    sum_x = RingSum(links, sx_out, sx_via, sx_got, x, (left, dp), (right, dp))
    gather_a.relay()
    pair_copy.wait_recv()

    def join(place, carry):
        for half in range(2):
            total = keep[place, half] + pair_got[place, half].astype(F32)
            keep[place, half] = total
            sx_out[place, half] = total.astype(BF16)
        return carry

    lax.fori_loop(0, 4, join, 0)
    sum_x.begin()
    hear(2)
    tell(3)
    gather_a.share()
    sum_x.relay()
    gather_b.begin()
    gather_a.last()
    sum_x.end()
    for half in range(2):
        total = part[half * 4] + keep[x, half] + sum_x.arrived(half)
        g_kv[me, half] = total.astype(BF16)
    gather_g = Gather(links, lambda d: g_kv.at[d], lambda d, h: g_kv.at[d, h], ring)
    gather_g.begin()
    gather_a.end()
    gather_b.relay()
    gather_b.share()
    gather_b.last()
    gather_g.relay()
    gather_b.end()

    def weigh(g_ref, out, columns):
        def tile(t, carry):
            cols = pl.ds(pl.multiple_of(t * 256, 256), 256)
            grads = g_ref[:, :, :, cols].reshape(2048, 256)
            term = dot(xt[...], grads, NN).astype(BF16)
            for k in range(4):
                for half in range(2):
                    out[k, half, :, cols] = term[k * 128 + half * 64 : k * 128 + half * 64 + 64]
            return carry

        lax.fori_loop(0, columns // 256, tile, 0)

    weigh(g_q, yq_out, 512)
    sum_yq = RingSum(links, yq_out, yq_via, yq_got, y, y_left, y_right)
    sum_yq.begin()
    gather_g.share()
    gather_g.last()
    sum_yq.relay()
    gather_g.end()
    weigh(g_kv, yk_out, 256)
    sum_yk = RingSum(links, yk_out, yk_via, yk_got, y, y_left, y_right)
    sum_yk.begin()

    def to_line(sums, own, out):
        for half in range(2):
            total = sums.out[y, half].astype(F32) + sums.arrived(half)
            for k in range(2):
                some = total[k * 32 : (k + 1) * 32]
                own[half * 2 + k] = some
                out[half * 2 + k] = some.astype(BF16)

    sum_yq.end()
    to_line(sum_yq, zq_own, zq_out)
    line_q = LineSum(links, zq_out, zq_got, zl, near)
    line_q.begin()
    sum_yk.relay()
    sum_yk.end()
    to_line(sum_yk, zk_own, zk_out)
    line_k = LineSum(links, zk_out, zk_got, zl, near)
    line_k.begin()
    hear(3)
    order = (4, 3, 5, 2, 6, 1, 7)

    def to_far(own, line, far_own, far_out, far_got):
        line.end()
        total = own[zl] + line.arrived()
        for k in range(8):
            some = total[k * 4 : (k + 1) * 4]
            far_own[k] = some
            far_out[k] = some.astype(BF16)
        sends = []
        for n, shift in enumerate(order):
            sends.append(links.copy(far_out.at[lax.rem(zh + shift, 8)], far_got.at[n], group(zh + shift)))
            sends[-1].start()
        return sends

    far_q = to_far(zq_own, line_q, fq_own, fq_out, fq_got)
    far_k = to_far(zk_own, line_k, fk_own, fk_out, fk_got)
    for sends, own, got, cols in ((far_q, fq_own, fq_got, slice(0, 512)), (far_k, fk_own, fk_got, slice(512, 768))):
        total = own[zh]
        for n in reversed(range(7)):
            sends[n].wait_recv()
            total = total + got[n].astype(F32)
        out_ref[:, cols] = total
    for made in links.sent:
        made.wait_send()
    assert links.count == COPIES


def body(layer_input, query_proj, key_proj, value_proj, out_grad, block_pos, doc_ids):
    hbm = pl.BlockSpec(memory_space=pl.ANY)

    def ring_buffers(half_rows, columns):
        return [
            pltpu.VMEM((4, 2, half_rows, columns), BF16),
            pltpu.VMEM((2, half_rows, columns), BF16),
            pltpu.VMEM((2, 2, half_rows, columns), BF16),
        ]

    def line_buffers(columns):
        return [
            pltpu.VMEM((4, 32, columns), F32),
            pltpu.VMEM((4, 32, columns), BF16),
            pltpu.VMEM((3, 32, columns), BF16),
        ]

    def far_buffers(columns):
        return [
            pltpu.VMEM((8, 4, columns), F32),
            pltpu.VMEM((8, 4, columns), BF16),
            pltpu.VMEM((7, 4, columns), BF16),
        ]

    return pl.pallas_call(
        kernel,
        out_shape=jax.ShapeDtypeStruct((4, 768), F32),
        in_specs=[hbm, hbm, hbm, hbm, hbm, hbm, hbm],
        out_specs=pl.BlockSpec(memory_space=pltpu.VMEM),
        scratch_shapes=[
            pltpu.SMEM((1, 16), jnp.int32),
            pltpu.SMEM((1, 16), jnp.int32),
            pltpu.VMEM((8, 2, BLK, 256), BF16),
            pltpu.VMEM((2, BLK, 512), BF16),
            pltpu.VMEM((2, BLK, 512), BF16),
            pltpu.VMEM((2048, 512), BF16),
            pltpu.VMEM((512, 2048), BF16),
            pltpu.VMEM((8, 2, BLK, 512), BF16),
            pltpu.VMEM((8, 2, BLK, 256), BF16),
            pltpu.SMEM((8,), jnp.int32),
            pltpu.SMEM((8,), F32),
            pltpu.SMEM((32,), jnp.int32),
            pltpu.VMEM((9, BLK, 256), F32),
            pltpu.VMEM((4, 2, BLK, 256), BF16),
            pltpu.VMEM((4, 2, BLK, 256), BF16),
            pltpu.VMEM((4, 2, BLK, 256), F32),
            *ring_buffers(BLK, 256),
            *ring_buffers(64, 512),
            *ring_buffers(64, 256),
            *line_buffers(512),
            *line_buffers(256),
            *far_buffers(512),
            *far_buffers(256),
            pltpu.SemaphoreType.DMA((7,)),
            pltpu.SemaphoreType.REGULAR((8,)),
            pltpu.SemaphoreType.DMA((COPIES,)),
            pltpu.SemaphoreType.DMA((COPIES,)),
        ],
        compiler_params=pltpu.CompilerParams(
            collective_id=0, has_side_effects=True, vmem_limit_bytes=56 * 1024 * 1024
        ),
    )(
        block_pos,
        doc_ids,
        layer_input.reshape(2048, 512),
        query_proj.reshape(2, BLK, 512),
        key_proj.reshape(2, BLK, HD),
        value_proj.reshape(2, BLK, HD),
        out_grad.reshape(2, BLK, 512),
    )


def solution(mesh):
    placed = (
        P("dp", None, "seq"),
        P("dp", "seq", None),
        P("dp", "seq", None),
        P("dp", "seq", None),
        P("dp", "seq", None),
        P("dp", None),
        P("dp", None),
    )
    return jax.shard_map(
        body, mesh=mesh, in_specs=placed, out_specs=P(("seq", "dp"), None), check_vma=False
    )
```

```python
import functools

import jax
import jax.numpy as jnp
from jax import lax
from jax.experimental import pallas as pl
from jax.experimental.pallas import tpu as pltpu
from jax.sharding import PartitionSpec as P

MESH = pl.DeviceIdType.MESH
F32 = jnp.float32
BF16 = jnp.bfloat16
FILL = -1e30
BLK = 128
HD = 128
CHUNKS = 3
COPIES = 4 * 7 + 5 + CHUNKS * (6 + 3 + 7)
NT = (((1,), (1,)), ((), ()))
NN = (((1,), (0,)), ((), ()))
TN = (((0,), (0,)), ((), ()))


def dot(a, b, dims):
    return lax.dot_general(a, b, dims, preferred_element_type=F32)


class Links:
    def __init__(self, send_sems, recv_sems):
        self.send_sems, self.recv_sems = send_sems, recv_sems
        self.count = 0
        self.sent = []

    def copy(self, src, dst, device):
        made = pltpu.make_async_remote_copy(
            src_ref=src,
            dst_ref=dst,
            send_sem=self.send_sems.at[self.count],
            recv_sem=self.recv_sems.at[self.count],
            device_id=device,
            device_id_type=MESH,
        )
        self.count += 1
        self.sent.append(made)
        return made


class Gather:
    def __init__(self, links, block, ring):
        me, mate, prev_same, prev_mate, far_same, dev_next, dev_pair = ring
        plan = [
            (me, dev_pair),
            (me, dev_next),
            (mate, dev_next),
            (prev_same, dev_next),
            (prev_same, dev_pair),
            (prev_mate, dev_pair),
            (far_same, dev_pair),
        ]
        self.c = [links.copy(block(d), block(d), device) for d, device in plan]

    def begin(self):
        self.c[1].start()
        self.c[0].start()

    def mate(self):
        self.c[0].wait_recv()
        self.c[2].start()

    def relay(self):
        self.c[1].wait_recv()
        self.c[3].start()
        self.c[4].start()

    def share(self):
        self.c[2].wait_recv()
        self.c[5].start()

    def last(self):
        self.c[3].wait_recv()
        self.c[6].start()

    def end(self):
        for k in (4, 5, 6):
            self.c[k].wait_recv()


class RingSum:
    def __init__(self, links, out, via, got, place, dev_left, dev_right):
        self.out, self.via, self.got = out, via, got
        self.place = place
        self.left, self.right = lax.rem(place + 3, 4), lax.rem(place + 1, 4)
        far = lax.rem(place + 2, 4)
        cp = links.copy
        self.c = [
            cp(out.at[far, 0], via.at[0], dev_right),
            cp(out.at[far, 1], via.at[1], dev_left),
            cp(out.at[self.right, 1], got.at[0, 1], dev_right),
            cp(out.at[self.left, 0], got.at[1, 0], dev_left),
            cp(out.at[self.right, 0], got.at[0, 0], dev_right),
            cp(out.at[self.left, 1], got.at[1, 1], dev_left),
        ]

    def begin(self):
        for k in range(4):
            self.c[k].start()

    def relay(self):
        for k, there in ((0, self.right), (1, self.left)):
            self.c[k].wait_recv()
            both = self.out[there, k].astype(F32) + self.via[k].astype(F32)
            self.out[there, k] = both.astype(BF16)
            self.c[4 + k].start()

    def end(self):
        for k in (2, 3, 4, 5):
            self.c[k].wait_recv()

    def arrived(self, half):
        return self.got[0, half].astype(F32) + self.got[1, half].astype(F32)


class LineSum:
    def __init__(self, links, out, got, place, device_of):
        self.got = got
        self.c = []
        for k in (1, 2, 3):
            there = lax.rem(place + k, 4)
            self.c.append(links.copy(out.at[there], got.at[k - 1], device_of(there)))

    def begin(self):
        for c in self.c:
            c.start()

    def end(self):
        for c in self.c:
            c.wait_recv()

    def arrived(self):
        return self.got[0].astype(F32) + self.got[1].astype(F32) + self.got[2].astype(F32)


def kernel(
    pos_hbm, doc_hbm, x_hbm, q_hbm, k_hbm, v_hbm, og_hbm, out_ref,
    pos_ref, doc_ref, kv, q_v, og_v, x_v, xt, g, key_at, bias_at, slot_at,
    part, pair_out, pair_got, keep, sx_out, sx_got,
    y_out, y_via, y_got, z_own, z_out, z_got, f_own, f_out, f_got, early,
    local_sems, known_sems, send_sems, recv_sems,
):
    me, dp = lax.axis_index("seq"), lax.axis_index("dp")
    x, c = me // 2, me % 2
    z, y = dp // 4, dp % 4
    zh, zl = z // 4, z % 4

    def at_x(place, core):
        return lax.rem(place, 4) * 2 + core

    left, right, far, pair = at_x(x + 3, c), at_x(x + 1, c), at_x(x + 2, c), at_x(x, 1 - c)
    step = 1 + 2 * c
    next_x, prev_x = x + step, x + 4 - step
    dev_next, dev_pair = (at_x(next_x, c), dp), (pair, dp)
    y_left = (me, z * 4 + lax.rem(y + 3, 4))
    y_right = (me, z * 4 + lax.rem(y + 1, 4))

    def near(place):
        return (me, (zh * 4 + place) * 4 + y)

    def group(place):
        return (me, (lax.rem(place, 8) * 4 + zl) * 4 + y)

    def at_z(shift):
        return (me, lax.rem(z + shift + 32, 32) * 4 + y)

    loads = [
        pltpu.make_async_copy(k_hbm, kv.at[me, :, :, pl.ds(0, HD)], local_sems.at[0]),
        pltpu.make_async_copy(v_hbm, kv.at[me, :, :, pl.ds(HD, HD)], local_sems.at[1]),
        pltpu.make_async_copy(x_hbm, x_v, local_sems.at[2]),
        pltpu.make_async_copy(q_hbm, q_v, local_sems.at[3]),
        pltpu.make_async_copy(og_hbm, og_v, local_sems.at[4]),
        pltpu.make_async_copy(pos_hbm, pos_ref, local_sems.at[5]),
        pltpu.make_async_copy(doc_hbm, doc_ref, local_sems.at[6]),
    ]
    for load in loads:
        load.start()

    barrier = pltpu.get_barrier_semaphore()
    peers = [(left, dp), (right, dp), (pair, dp), y_left, y_right, at_z(-1), at_z(1)]
    for peer in peers:
        pl.semaphore_signal(barrier, inc=1, device_id=peer, device_id_type=MESH)
    pl.semaphore_wait(barrier, len(peers))

    links = Links(send_sems, recv_sems)
    ring = (me, pair, at_x(prev_x, c), at_x(prev_x, 1 - c), far, dev_next, dev_pair)
    gather_kv = Gather(links, lambda d: kv.at[d], ring)
    loads[0].wait()
    loads[1].wait()
    gather_kv.begin()

    def tell(r):
        for side, way in enumerate((1, -1)):
            pl.semaphore_signal(
                known_sems.at[2 * r + side], inc=1, device_id=at_z(way * 2**r), device_id_type=MESH
            )

    def hear(r):
        for side in range(2):
            pl.semaphore_wait(known_sems.at[2 * r + side], 1)

    tell(0)
    loads[5].wait()
    loads[6].wait()

    hits = []
    for q in range(2):
        mine = pos_ref[0, me * 2 + q]
        doc = doc_ref[0, mine]
        key_at[q * 4] = me * 2 + q
        bias_at[q * 4] = jnp.float32(0.0)
        for j in range(1, 4):
            want = jnp.maximum(mine - j, 0)
            live = jnp.logical_and(mine >= j, doc_ref[0, want] == doc)
            spot = jnp.int32(0)
            for s in range(16):
                spot = jnp.where(pos_ref[0, s] == want, jnp.int32(s), spot)
            key_at[q * 4 + j] = spot
            bias_at[q * 4 + j] = jnp.where(live, jnp.float32(0.0), jnp.float32(FILL))
            hits.append((q, q * 4 + j, jnp.where(live, spot, jnp.int32(-1))))
    for s in range(16):
        for q in range(2):
            slot = jnp.int32(8)
            for owner, number, spot in hits:
                if owner == q:
                    slot = jnp.where(spot == s, jnp.int32(number), slot)
            slot_at[q * 16 + s] = slot

    gather_kv.mate()

    loads[2].wait()
    new = lax.broadcasted_iota(jnp.int32, (512, 512), 0)
    old = lax.broadcasted_iota(jnp.int32, (512, 512), 1)
    source = (new // 4 % 8) * 64 + (new // 32 % 4) * 16 + (new // 128) * 4 + new % 4
    one_hot = (old == source).astype(F32).astype(BF16)

    def flip(t, carry):
        at = pl.multiple_of(t * 256, 256)
        xt[:, pl.ds(at, 256)] = dot(one_hot, x_v[pl.ds(at, 256), :], NT).astype(BF16)
        return carry

    lax.fori_loop(0, 4, flip, 0)
    gather_kv.relay()
    lax.fori_loop(4, 8, flip, 0)
    gather_kv.share()
    hear(0)
    tell(1)
    part[...] = jnp.zeros_like(part)
    loads[3].wait()
    loads[4].wait()
    gather_kv.last()
    hear(1)
    tell(2)
    gather_kv.end()

    scaling = HD ** (-0.5)
    key_row = lax.broadcasted_iota(jnp.int32, (BLK, 2 * BLK), 0)
    query_col = lax.broadcasted_iota(jnp.int32, (BLK, 2 * BLK), 1) % BLK
    causal = key_row <= query_col

    def attend(step, carry):
        pair_of_heads, q = step // 2, step % 2
        cols = pl.ds(pl.multiple_of(pair_of_heads * 256, 256), 256)
        q_two, og_two = q_v[q, :, cols], og_v[q, :, cols]
        queries = jnp.concatenate([q_two[:, :HD], q_two[:, HD:]], axis=0)
        grads = jnp.concatenate([og_two[:, :HD], og_two[:, HD:]], axis=0)
        blocks = []
        for j in range(4):
            spot = key_at[q * 4 + j]
            blocks.append(kv[spot // 2, spot % 2])
        both = jnp.concatenate(blocks, axis=0)
        keys, values = both[:, :HD], both[:, HD:]
        scores = dot(keys, queries, NT) * scaling
        masked = [jnp.where(causal, scores[:BLK], FILL)]
        for j in range(1, 4):
            masked.append(scores[j * BLK : (j + 1) * BLK] + bias_at[q * 4 + j])
        scores = jnp.concatenate(masked, axis=0)
        peak = jnp.max(scores, axis=0, keepdims=True)
        weights = jnp.exp(scores - peak)
        probs = weights * (1.0 / jnp.sum(weights, axis=0, keepdims=True))
        probs_b = probs.astype(BF16)
        dprobs = dot(values, grads, NT)
        delta = jnp.sum(probs_b.astype(F32) * dprobs, axis=0, keepdims=True)
        dscores = (probs * (dprobs - delta)).astype(BF16)
        dq = (dot(dscores, keys, TN) * scaling).astype(BF16)
        g[pair_of_heads, me, q] = jnp.concatenate([dq[:BLK], dq[BLK:]], axis=1)
        dk = dot(dscores, queries, NN) * scaling
        dv = dot(probs_b, grads, NN)
        for j in range(4):
            block = slice(j * BLK, (j + 1) * BLK)
            part[q * 4 + j, :, :HD] += dk[block]
            part[q * 4 + j, :, HD:] += dv[block]
        return carry

    gather_a, gather_b, gather_c = (Gather(links, lambda d, n=n: g.at[n, d], ring) for n in range(CHUNKS))
    lax.fori_loop(0, 2, attend, 0, unroll=True)
    gather_a.begin()
    lax.fori_loop(2, 4, attend, 0, unroll=True)
    gather_a.mate()

    def roles(core):
        ahead = x + 1 + 2 * core
        return at_x(x + 2, core), at_x(ahead, 1 - core), at_x(ahead, core), at_x(x, core)

    def to_block(device, half):
        s = device * 2 + half
        return part[slot_at[s]] + part[slot_at[16 + s]]

    for r, device in enumerate(roles(1 - c)):
        for half in range(2):
            pair_out[r, half] = to_block(device, half).astype(BF16)
    pair_copy = links.copy(pair_out, pair_got, dev_pair)
    pair_copy.start()
    for r, device in enumerate(roles(c)):
        for half in range(2):
            keep[r, half] = to_block(device, half)
    sum_far = links.copy(sx_out.at[0], sx_got.at[0], dev_next)
    sum_other = links.copy(sx_out.at[1], sx_got.at[1], dev_next)
    sum_same = links.copy(sx_out.at[2], sx_got.at[2], dev_next)
    sum_cross = links.copy(sx_got.at[1], sx_got.at[3], dev_pair)
    pair_copy.wait_recv()
    for r in range(4):
        for half in range(2):
            total = keep[r, half] + pair_got[r, half].astype(F32)
            if r < 2:
                sx_out[r, half] = total.astype(BF16)
            else:
                keep[r, half] = total
        if r == 0:
            sum_far.start()
        if r == 1:
            sum_other.start()
    hear(2)
    tell(3)
    gather_a.relay()
    sum_far.wait_recv()
    for half in range(2):
        sx_out[2, half] = (keep[2, half] + sx_got[0, half].astype(F32)).astype(BF16)
    sum_same.start()
    gather_b.begin()
    gather_a.share()
    sum_other.wait_recv()
    sum_cross.start()
    gather_b.mate()
    sum_same.wait_recv()
    sum_cross.wait_recv()
    for half in range(2):
        moved = sx_got[2, half].astype(F32) + sx_got[3, half].astype(F32)
        g[2, me, half] = (part[half * 4] + keep[3, half] + moved).astype(BF16)
    gather_c.begin()
    gather_a.last()

    def product(n, devices):
        total = None
        for device in devices:
            tokens = pl.ds(pl.multiple_of(device * 256, 256), 256)
            term = dot(xt[:, tokens], g[n, device].reshape(256, 256), NN)
            total = term if total is None else total + term
        return total

    def weigh(n, term=None):
        if term is None:
            term = dot(xt[...], g[n].reshape(2048, 256), NN)
        term = term.astype(BF16)
        for k in range(4):
            for half in range(2):
                at = k * 128 + half * 64
                y_out[n, k, half] = term[at : at + 64]
        sums = RingSum(links, y_out.at[n], y_via.at[n], y_got.at[n], y, y_left, y_right)
        sums.begin()
        return sums

    def to_line(n, sums):
        sums.end()
        for half in range(2):
            total = y_out[n, y, half].astype(F32) + sums.arrived(half)
            for k in range(2):
                some = total[k * 32 : (k + 1) * 32]
                z_own[n, half * 2 + k] = some
                z_out[n, half * 2 + k] = some.astype(BF16)
        line = LineSum(links, z_out.at[n], z_got.at[n], zl, near)
        line.begin()
        return line

    order = (4, 3, 5, 2, 6, 1, 7)

    def to_far(n, line):
        line.end()
        total = z_own[n, zl] + line.arrived()
        for k in range(8):
            some = total[k * 4 : (k + 1) * 4]
            f_own[n, k] = some
            f_out[n, k] = some.astype(BF16)
        sends = []
        for i, shift in enumerate(order):
            there = lax.rem(zh + shift, 8)
            sends.append(links.copy(f_out.at[n, there], f_got.at[n, i], group(there)))
            sends[-1].start()
        return sends

    gather_c.mate()
    gather_b.relay()
    gather_c.relay()
    gather_a.end()
    sum_a = weigh(0)
    gather_b.share()
    gather_c.share()
    gather_b.last()
    sum_a.relay()
    early[...] = product(2, (me, pair, at_x(prev_x, c), at_x(prev_x, 1 - c)))
    gather_c.last()
    gather_b.end()
    sum_b = weigh(1)
    gather_c.end()
    sum_c = weigh(2, early[...] + product(2, (at_x(next_x, c), at_x(next_x, 1 - c), far, at_x(x + 2, 1 - c))))
    sum_b.relay()
    sum_c.relay()
    line_a = to_line(0, sum_a)
    line_b = to_line(1, sum_b)
    line_c = to_line(2, sum_c)
    hear(3)
    far_a = to_far(0, line_a)
    far_b = to_far(1, line_b)
    far_c = to_far(2, line_c)
    for n, sends in enumerate((far_a, far_b, far_c)):
        total = f_own[n, zh]
        for i in reversed(range(7)):
            sends[i].wait_recv()
            total = total + f_got[n, i].astype(F32)
        out_ref[:, n * 256 : (n + 1) * 256] = total
    for made in links.sent:
        made.wait_send()
    assert links.count == COPIES


def body(layer_input, query_proj, key_proj, value_proj, out_grad, block_pos, doc_ids):
    hbm = pl.BlockSpec(memory_space=pl.ANY)

    return pl.pallas_call(
        kernel,
        out_shape=jax.ShapeDtypeStruct((4, 768), F32),
        in_specs=[hbm, hbm, hbm, hbm, hbm, hbm, hbm],
        out_specs=pl.BlockSpec(memory_space=pltpu.VMEM),
        scratch_shapes=[
            pltpu.SMEM((1, 16), jnp.int32),
            pltpu.SMEM((1, 16), jnp.int32),
            pltpu.VMEM((8, 2, BLK, 256), BF16),
            pltpu.VMEM((2, BLK, 512), BF16),
            pltpu.VMEM((2, BLK, 512), BF16),
            pltpu.VMEM((2048, 512), BF16),
            pltpu.VMEM((512, 2048), BF16),
            pltpu.VMEM((CHUNKS, 8, 2, BLK, 256), BF16),
            pltpu.SMEM((8,), jnp.int32),
            pltpu.SMEM((8,), F32),
            pltpu.SMEM((32,), jnp.int32),
            pltpu.VMEM((9, BLK, 256), F32),
            pltpu.VMEM((4, 2, BLK, 256), BF16),
            pltpu.VMEM((4, 2, BLK, 256), BF16),
            pltpu.VMEM((4, 2, BLK, 256), F32),
            pltpu.VMEM((3, 2, BLK, 256), BF16),
            pltpu.VMEM((4, 2, BLK, 256), BF16),
            pltpu.VMEM((CHUNKS, 4, 2, 64, 256), BF16),
            pltpu.VMEM((CHUNKS, 2, 64, 256), BF16),
            pltpu.VMEM((CHUNKS, 2, 2, 64, 256), BF16),
            pltpu.VMEM((CHUNKS, 4, 32, 256), F32),
            pltpu.VMEM((CHUNKS, 4, 32, 256), BF16),
            pltpu.VMEM((CHUNKS, 3, 32, 256), BF16),
            pltpu.VMEM((CHUNKS, 8, 4, 256), F32),
            pltpu.VMEM((CHUNKS, 8, 4, 256), BF16),
            pltpu.VMEM((CHUNKS, 7, 4, 256), BF16),
            pltpu.VMEM((512, 256), F32),
            pltpu.SemaphoreType.DMA((7,)),
            pltpu.SemaphoreType.REGULAR((8,)),
            pltpu.SemaphoreType.DMA((COPIES,)),
            pltpu.SemaphoreType.DMA((COPIES,)),
        ],
        compiler_params=pltpu.CompilerParams(
            collective_id=0, has_side_effects=True, vmem_limit_bytes=56 * 1024 * 1024
        ),
    )(
        block_pos,
        doc_ids,
        layer_input.reshape(2048, 512),
        query_proj.reshape(2, BLK, 512),
        key_proj.reshape(2, BLK, HD),
        value_proj.reshape(2, BLK, HD),
        out_grad.reshape(2, BLK, 512),
    )


def solution(mesh):
    placed = (
        P("dp", None, "seq"),
        P("dp", "seq", None),
        P("dp", "seq", None),
        P("dp", "seq", None),
        P("dp", "seq", None),
        P("dp", None),
        P("dp", None),
    )
    return jax.shard_map(
        body, mesh=mesh, in_specs=placed, out_specs=P(("seq", "dp"), None), check_vma=False
    )
```

```python
import functools

import jax
import jax.numpy as jnp
from jax import lax
from jax.experimental import pallas as pl
from jax.experimental.pallas import tpu as pltpu
from jax.sharding import PartitionSpec as P

MESH = pl.DeviceIdType.MESH
F32 = jnp.float32
BF16 = jnp.bfloat16
FILL = -1e30
BLK = 128
HD = 128
CHUNKS = 3
COPIES = 5 * 7 + 5 + CHUNKS * (6 + 3 + 7)
NT = (((1,), (1,)), ((), ()))
NN = (((1,), (0,)), ((), ()))
TN = (((0,), (0,)), ((), ()))


def dot(a, b, dims):
    return lax.dot_general(a, b, dims, preferred_element_type=F32)


class Links:
    def __init__(self, send_sems, recv_sems):
        self.send_sems, self.recv_sems = send_sems, recv_sems
        self.count = 0
        self.sent = []

    def copy(self, src, dst, device):
        made = pltpu.make_async_remote_copy(
            src_ref=src,
            dst_ref=dst,
            send_sem=self.send_sems.at[self.count],
            recv_sem=self.recv_sems.at[self.count],
            device_id=device,
            device_id_type=MESH,
        )
        self.count += 1
        self.sent.append(made)
        return made


class Gather:
    def __init__(self, links, block, ring):
        me, mate, prev_same, prev_mate, far_same, dev_next, dev_pair = ring
        plan = [
            (me, dev_pair),
            (me, dev_next),
            (mate, dev_next),
            (prev_same, dev_next),
            (prev_same, dev_pair),
            (prev_mate, dev_pair),
            (far_same, dev_pair),
        ]
        self.c = [links.copy(block(d), block(d), device) for d, device in plan]

    def begin(self):
        self.c[1].start()
        self.c[0].start()

    def mate(self):
        self.c[0].wait_recv()
        self.c[2].start()

    def relay(self):
        self.c[1].wait_recv()
        self.c[3].start()
        self.c[4].start()

    def share(self):
        self.c[2].wait_recv()
        self.c[5].start()

    def last(self):
        self.c[3].wait_recv()
        self.c[6].start()

    def end(self):
        for k in (4, 5, 6):
            self.c[k].wait_recv()


class RingSum:
    def __init__(self, links, out, via, got, place, dev_left, dev_right):
        self.out, self.via, self.got = out, via, got
        self.place = place
        self.left, self.right = lax.rem(place + 3, 4), lax.rem(place + 1, 4)
        far = lax.rem(place + 2, 4)
        cp = links.copy
        self.c = [
            cp(out.at[far, 0], via.at[0], dev_right),
            cp(out.at[far, 1], via.at[1], dev_left),
            cp(out.at[self.right, 1], got.at[0, 1], dev_right),
            cp(out.at[self.left, 0], got.at[1, 0], dev_left),
            cp(out.at[self.right, 0], got.at[0, 0], dev_right),
            cp(out.at[self.left, 1], got.at[1, 1], dev_left),
        ]

    def begin(self):
        for k in range(4):
            self.c[k].start()

    def relay(self):
        for k, there in ((0, self.right), (1, self.left)):
            self.c[k].wait_recv()
            both = self.out[there, k].astype(F32) + self.via[k].astype(F32)
            self.out[there, k] = both.astype(BF16)
            self.c[4 + k].start()

    def end(self):
        for k in (2, 3, 4, 5):
            self.c[k].wait_recv()

    def arrived(self, half):
        return self.got[0, half].astype(F32) + self.got[1, half].astype(F32)


class LineSum:
    def __init__(self, links, out, got, place, device_of):
        self.got = got
        self.c = []
        for k in (1, 2, 3):
            there = lax.rem(place + k, 4)
            self.c.append(links.copy(out.at[there], got.at[k - 1], device_of(there)))

    def begin(self):
        for c in self.c:
            c.start()

    def end(self):
        for c in self.c:
            c.wait_recv()

    def arrived(self):
        return self.got[0].astype(F32) + self.got[1].astype(F32) + self.got[2].astype(F32)


def kernel(
    pos_hbm, doc_hbm, x_hbm, q_hbm, k_hbm, v_hbm, og_hbm, out_ref,
    pos_ref, doc_ref, k_all, v_all, q_v, og_v, x_v, xt, g, key_at, bias_at, slot_at,
    part, pair_out, pair_got, keep, sx_out, sx_got,
    y_out, y_via, y_got, z_own, z_out, z_got, f_own, f_out, f_got, early, probs_at,
    local_sems, known_sems, send_sems, recv_sems,
):
    me, dp = lax.axis_index("seq"), lax.axis_index("dp")
    x, c = me // 2, me % 2
    z, y = dp // 4, dp % 4
    zh, zl = z // 4, z % 4

    def at_x(place, core):
        return lax.rem(place, 4) * 2 + core

    left, right, far, pair = at_x(x + 3, c), at_x(x + 1, c), at_x(x + 2, c), at_x(x, 1 - c)
    step = 1 + 2 * c
    next_x, prev_x = x + step, x + 4 - step
    dev_next, dev_pair = (at_x(next_x, c), dp), (pair, dp)
    y_left = (me, z * 4 + lax.rem(y + 3, 4))
    y_right = (me, z * 4 + lax.rem(y + 1, 4))

    def near(place):
        return (me, (zh * 4 + place) * 4 + y)

    def group(place):
        return (me, (lax.rem(place, 8) * 4 + zl) * 4 + y)

    def at_z(shift):
        return (me, lax.rem(z + shift + 32, 32) * 4 + y)

    loads = [
        pltpu.make_async_copy(k_hbm, k_all.at[me], local_sems.at[0]),
        pltpu.make_async_copy(v_hbm, v_all.at[me], local_sems.at[1]),
        pltpu.make_async_copy(x_hbm, x_v, local_sems.at[2]),
        pltpu.make_async_copy(q_hbm, q_v, local_sems.at[3]),
        pltpu.make_async_copy(og_hbm, og_v, local_sems.at[4]),
        pltpu.make_async_copy(pos_hbm, pos_ref, local_sems.at[5]),
        pltpu.make_async_copy(doc_hbm, doc_ref, local_sems.at[6]),
    ]
    for load in loads:
        load.start()

    barrier = pltpu.get_barrier_semaphore()
    peers = [(left, dp), (right, dp), (pair, dp), y_left, y_right, at_z(-1), at_z(1)]
    for peer in peers:
        pl.semaphore_signal(barrier, inc=1, device_id=peer, device_id_type=MESH)
    pl.semaphore_wait(barrier, len(peers))

    links = Links(send_sems, recv_sems)
    ring = (me, pair, at_x(prev_x, c), at_x(prev_x, 1 - c), far, dev_next, dev_pair)
    gather_k = Gather(links, lambda d: k_all.at[d], ring)
    gather_v = Gather(links, lambda d: v_all.at[d], ring)
    loads[0].wait()
    gather_k.begin()
    loads[1].wait()
    gather_v.begin()

    def tell(r):
        for side, way in enumerate((1, -1)):
            pl.semaphore_signal(
                known_sems.at[2 * r + side], inc=1, device_id=at_z(way * 2**r), device_id_type=MESH
            )

    def hear(r):
        for side in range(2):
            pl.semaphore_wait(known_sems.at[2 * r + side], 1)

    tell(0)
    loads[5].wait()
    loads[6].wait()

    hits = []
    for q in range(2):
        mine = pos_ref[0, me * 2 + q]
        doc = doc_ref[0, mine]
        key_at[q * 4] = me * 2 + q
        bias_at[q * 4] = jnp.float32(0.0)
        for j in range(1, 4):
            want = jnp.maximum(mine - j, 0)
            live = jnp.logical_and(mine >= j, doc_ref[0, want] == doc)
            spot = jnp.int32(0)
            for s in range(16):
                spot = jnp.where(pos_ref[0, s] == want, jnp.int32(s), spot)
            key_at[q * 4 + j] = spot
            bias_at[q * 4 + j] = jnp.where(live, jnp.float32(0.0), jnp.float32(FILL))
            hits.append((q, q * 4 + j, jnp.where(live, spot, jnp.int32(-1))))
    for s in range(16):
        for q in range(2):
            slot = jnp.int32(8)
            for owner, number, spot in hits:
                if owner == q:
                    slot = jnp.where(spot == s, jnp.int32(number), slot)
            slot_at[q * 16 + s] = slot

    gather_k.mate()
    gather_v.mate()

    loads[2].wait()
    new = lax.broadcasted_iota(jnp.int32, (512, 512), 0)
    old = lax.broadcasted_iota(jnp.int32, (512, 512), 1)
    source = (new // 4 % 8) * 64 + (new // 32 % 4) * 16 + (new // 128) * 4 + new % 4
    one_hot = (old == source).astype(F32).astype(BF16)

    def flip(t, carry):
        at = pl.multiple_of(t * 256, 256)
        xt[:, pl.ds(at, 256)] = dot(one_hot, x_v[pl.ds(at, 256), :], NT).astype(BF16)
        return carry

    lax.fori_loop(0, 2, flip, 0)
    gather_k.relay()
    gather_v.relay()
    hear(0)
    tell(1)
    lax.fori_loop(2, 5, flip, 0)
    gather_k.share()
    gather_v.share()
    lax.fori_loop(5, 7, flip, 0)
    gather_k.last()
    gather_v.last()
    hear(1)
    tell(2)
    lax.fori_loop(7, 8, flip, 0)
    part[...] = jnp.zeros_like(part)
    loads[3].wait()
    loads[4].wait()
    gather_k.end()

    scaling = HD ** (-0.5)
    key_row = lax.broadcasted_iota(jnp.int32, (BLK, 2 * BLK), 0)
    query_col = lax.broadcasted_iota(jnp.int32, (BLK, 2 * BLK), 1) % BLK
    causal = key_row <= query_col

    def operands(number):
        pair_of_heads, q = number // 2, number % 2
        cols = pl.ds(pl.multiple_of(pair_of_heads * 256, 256), 256)
        return pair_of_heads, q, cols

    def stacked(two):
        return jnp.concatenate([two[:, :HD], two[:, HD:]], axis=0)

    def four_blocks(ref, q):
        spots = [key_at[q * 4 + j] for j in range(4)]
        return jnp.concatenate([ref[spot // 2, spot % 2] for spot in spots], axis=0)

    def weigh_keys(number, carry):
        _, q, cols = operands(number)
        scores = dot(four_blocks(k_all, q), stacked(q_v[q, :, cols]), NT) * scaling
        masked = [jnp.where(causal, scores[:BLK], FILL)]
        for j in range(1, 4):
            masked.append(scores[j * BLK : (j + 1) * BLK] + bias_at[q * 4 + j])
        scores = jnp.concatenate(masked, axis=0)
        peak = jnp.max(scores, axis=0, keepdims=True)
        weights = jnp.exp(scores - peak)
        probs_at[number] = weights * (1.0 / jnp.sum(weights, axis=0, keepdims=True))
        return carry

    def attend(number, carry):
        pair_of_heads, q, cols = operands(number)
        queries, grads = stacked(q_v[q, :, cols]), stacked(og_v[q, :, cols])
        keys, values = four_blocks(k_all, q), four_blocks(v_all, q)
        probs = probs_at[number]
        probs_b = probs.astype(BF16)
        dprobs = dot(values, grads, NT)
        delta = jnp.sum(probs_b.astype(F32) * dprobs, axis=0, keepdims=True)
        dscores = (probs * (dprobs - delta)).astype(BF16)
        dq = (dot(dscores, keys, TN) * scaling).astype(BF16)
        g[pair_of_heads, me, q] = jnp.concatenate([dq[:BLK], dq[BLK:]], axis=1)
        dk = dot(dscores, queries, NN) * scaling
        dv = dot(probs_b, grads, NN)
        for j in range(4):
            block = slice(j * BLK, (j + 1) * BLK)
            part[q * 4 + j, :, :HD] += dk[block]
            part[q * 4 + j, :, HD:] += dv[block]
        return carry

    gather_a, gather_b, gather_c = (Gather(links, lambda d, n=n: g.at[n, d], ring) for n in range(CHUNKS))
    lax.fori_loop(0, 4, weigh_keys, 0, unroll=2)
    gather_v.end()
    lax.fori_loop(0, 2, attend, 0, unroll=True)
    gather_a.begin()
    lax.fori_loop(2, 4, attend, 0, unroll=True)
    gather_a.mate()

    def roles(core):
        ahead = x + 1 + 2 * core
        return at_x(x + 2, core), at_x(ahead, 1 - core), at_x(ahead, core), at_x(x, core)

    def to_block(device, half):
        s = device * 2 + half
        return part[slot_at[s]] + part[slot_at[16 + s]]

    for r, device in enumerate(roles(1 - c)):
        for half in range(2):
            pair_out[r, half] = to_block(device, half).astype(BF16)
    pair_copy = links.copy(pair_out, pair_got, dev_pair)
    pair_copy.start()
    for r, device in enumerate(roles(c)):
        for half in range(2):
            keep[r, half] = to_block(device, half)
    sum_far = links.copy(sx_out.at[0], sx_got.at[0], dev_next)
    sum_other = links.copy(sx_out.at[1], sx_got.at[1], dev_next)
    sum_same = links.copy(sx_out.at[2], sx_got.at[2], dev_next)
    sum_cross = links.copy(sx_got.at[1], sx_got.at[3], dev_pair)
    pair_copy.wait_recv()
    for r in range(4):
        for half in range(2):
            total = keep[r, half] + pair_got[r, half].astype(F32)
            if r < 2:
                sx_out[r, half] = total.astype(BF16)
            else:
                keep[r, half] = total
        if r == 0:
            sum_far.start()
        if r == 1:
            sum_other.start()
    hear(2)
    tell(3)
    gather_a.relay()
    sum_far.wait_recv()
    for half in range(2):
        sx_out[2, half] = (keep[2, half] + sx_got[0, half].astype(F32)).astype(BF16)
    sum_same.start()
    gather_b.begin()
    gather_a.share()
    sum_other.wait_recv()
    sum_cross.start()
    gather_b.mate()
    sum_same.wait_recv()
    sum_cross.wait_recv()
    for half in range(2):
        moved = sx_got[2, half].astype(F32) + sx_got[3, half].astype(F32)
        g[2, me, half] = (part[half * 4] + keep[3, half] + moved).astype(BF16)
    gather_c.begin()
    gather_a.last()

    def product(n, devices):
        total = None
        for device in devices:
            tokens = pl.ds(pl.multiple_of(device * 256, 256), 256)
            term = dot(xt[:, tokens], g[n, device].reshape(256, 256), NN)
            total = term if total is None else total + term
        return total

    def weigh(n, term=None):
        if term is None:
            term = dot(xt[...], g[n].reshape(2048, 256), NN)
        term = term.astype(BF16)
        for k in range(4):
            for half in range(2):
                at = k * 128 + half * 64
                y_out[n, k, half] = term[at : at + 64]
        sums = RingSum(links, y_out.at[n], y_via.at[n], y_got.at[n], y, y_left, y_right)
        sums.begin()
        return sums

    def to_line(n, sums):
        sums.end()
        for half in range(2):
            total = y_out[n, y, half].astype(F32) + sums.arrived(half)
            for k in range(2):
                some = total[k * 32 : (k + 1) * 32]
                z_own[n, half * 2 + k] = some
                z_out[n, half * 2 + k] = some.astype(BF16)
        line = LineSum(links, z_out.at[n], z_got.at[n], zl, near)
        line.begin()
        return line

    order = (4, 3, 5, 2, 6, 1, 7)

    def to_far(n, line):
        line.end()
        total = z_own[n, zl] + line.arrived()
        for k in range(8):
            some = total[k * 4 : (k + 1) * 4]
            f_own[n, k] = some
            f_out[n, k] = some.astype(BF16)
        sends = []
        for i, shift in enumerate(order):
            there = lax.rem(zh + shift, 8)
            sends.append(links.copy(f_out.at[n, there], f_got.at[n, i], group(there)))
            sends[-1].start()
        return sends

    gather_c.mate()
    gather_b.relay()
    gather_a.end()
    sum_a = weigh(0)
    gather_c.relay()
    gather_b.share()
    gather_c.share()
    gather_b.last()
    sum_a.relay()
    early[...] = product(2, (me, pair, at_x(prev_x, c), at_x(prev_x, 1 - c)))
    gather_c.last()
    gather_b.end()
    sum_b = weigh(1)
    gather_c.end()
    sum_c = weigh(2, early[...] + product(2, (at_x(next_x, c), at_x(next_x, 1 - c), far, at_x(x + 2, 1 - c))))
    sum_b.relay()
    sum_c.relay()
    line_a = to_line(0, sum_a)
    line_b = to_line(1, sum_b)
    line_c = to_line(2, sum_c)
    hear(3)
    far_a = to_far(0, line_a)
    far_b = to_far(1, line_b)
    far_c = to_far(2, line_c)
    for n, sends in enumerate((far_a, far_b, far_c)):
        total = f_own[n, zh]
        for i in reversed(range(7)):
            sends[i].wait_recv()
            total = total + f_got[n, i].astype(F32)
        out_ref[:, n * 256 : (n + 1) * 256] = total
    for made in links.sent:
        made.wait_send()
    assert links.count == COPIES


def body(layer_input, query_proj, key_proj, value_proj, out_grad, block_pos, doc_ids):
    hbm = pl.BlockSpec(memory_space=pl.ANY)

    return pl.pallas_call(
        kernel,
        out_shape=jax.ShapeDtypeStruct((4, 768), F32),
        in_specs=[hbm, hbm, hbm, hbm, hbm, hbm, hbm],
        out_specs=pl.BlockSpec(memory_space=pltpu.VMEM),
        scratch_shapes=[
            pltpu.SMEM((1, 16), jnp.int32),
            pltpu.SMEM((1, 16), jnp.int32),
            pltpu.VMEM((8, 2, BLK, HD), BF16),
            pltpu.VMEM((8, 2, BLK, HD), BF16),
            pltpu.VMEM((2, BLK, 512), BF16),
            pltpu.VMEM((2, BLK, 512), BF16),
            pltpu.VMEM((2048, 512), BF16),
            pltpu.VMEM((512, 2048), BF16),
            pltpu.VMEM((CHUNKS, 8, 2, BLK, 256), BF16),
            pltpu.SMEM((8,), jnp.int32),
            pltpu.SMEM((8,), F32),
            pltpu.SMEM((32,), jnp.int32),
            pltpu.VMEM((9, BLK, 256), F32),
            pltpu.VMEM((4, 2, BLK, 256), BF16),
            pltpu.VMEM((4, 2, BLK, 256), BF16),
            pltpu.VMEM((4, 2, BLK, 256), F32),
            pltpu.VMEM((3, 2, BLK, 256), BF16),
            pltpu.VMEM((4, 2, BLK, 256), BF16),
            pltpu.VMEM((CHUNKS, 4, 2, 64, 256), BF16),
            pltpu.VMEM((CHUNKS, 2, 64, 256), BF16),
            pltpu.VMEM((CHUNKS, 2, 2, 64, 256), BF16),
            pltpu.VMEM((CHUNKS, 4, 32, 256), F32),
            pltpu.VMEM((CHUNKS, 4, 32, 256), BF16),
            pltpu.VMEM((CHUNKS, 3, 32, 256), BF16),
            pltpu.VMEM((CHUNKS, 8, 4, 256), F32),
            pltpu.VMEM((CHUNKS, 8, 4, 256), BF16),
            pltpu.VMEM((CHUNKS, 7, 4, 256), BF16),
            pltpu.VMEM((512, 256), F32),
            pltpu.VMEM((4, 512, 256), F32),
            pltpu.SemaphoreType.DMA((7,)),
            pltpu.SemaphoreType.REGULAR((8,)),
            pltpu.SemaphoreType.DMA((COPIES,)),
            pltpu.SemaphoreType.DMA((COPIES,)),
        ],
        compiler_params=pltpu.CompilerParams(
            collective_id=0, has_side_effects=True, vmem_limit_bytes=56 * 1024 * 1024
        ),
    )(
        block_pos,
        doc_ids,
        layer_input.reshape(2048, 512),
        query_proj.reshape(2, BLK, 512),
        key_proj.reshape(2, BLK, HD),
        value_proj.reshape(2, BLK, HD),
        out_grad.reshape(2, BLK, 512),
    )


def solution(mesh):
    placed = (
        P("dp", None, "seq"),
        P("dp", "seq", None),
        P("dp", "seq", None),
        P("dp", "seq", None),
        P("dp", "seq", None),
        P("dp", None),
        P("dp", None),
    )
    return jax.shard_map(
        body, mesh=mesh, in_specs=placed, out_specs=P(("seq", "dp"), None), check_vma=False
    )
```

```python
import functools

import jax
import jax.numpy as jnp
from jax import lax
from jax.experimental import pallas as pl
from jax.experimental.pallas import tpu as pltpu
from jax.sharding import PartitionSpec as P

MESH = pl.DeviceIdType.MESH
F32 = jnp.float32
BF16 = jnp.bfloat16
FILL = -1e30
BLK = 128
HD = 128
CHUNKS = 3
COPIES = 6 * 7 + 5 + CHUNKS * (6 + 3 + 7)
NT = (((1,), (1,)), ((), ()))
NN = (((1,), (0,)), ((), ()))
TN = (((0,), (0,)), ((), ()))


def dot(a, b, dims):
    return lax.dot_general(a, b, dims, preferred_element_type=F32)


class Links:
    def __init__(self, send_sems, recv_sems):
        self.send_sems, self.recv_sems = send_sems, recv_sems
        self.count = 0
        self.sent = []

    def copy(self, src, dst, device):
        made = pltpu.make_async_remote_copy(
            src_ref=src,
            dst_ref=dst,
            send_sem=self.send_sems.at[self.count],
            recv_sem=self.recv_sems.at[self.count],
            device_id=device,
            device_id_type=MESH,
        )
        self.count += 1
        self.sent.append(made)
        return made


class Gather:
    def __init__(self, links, block, ring):
        me, mate, prev_same, prev_mate, far_same, dev_next, dev_pair = ring
        plan = [
            (me, dev_pair),
            (me, dev_next),
            (mate, dev_next),
            (prev_same, dev_next),
            (prev_same, dev_pair),
            (prev_mate, dev_pair),
            (far_same, dev_pair),
        ]
        self.c = [links.copy(block(d), block(d), device) for d, device in plan]

    def begin(self):
        self.c[1].start()
        self.c[0].start()

    def mate(self):
        self.c[0].wait_recv()
        self.c[2].start()

    def relay(self):
        self.c[1].wait_recv()
        self.c[3].start()
        self.c[4].start()

    def share(self):
        self.c[2].wait_recv()
        self.c[5].start()

    def last(self):
        self.c[3].wait_recv()
        self.c[6].start()

    def end(self):
        for k in (4, 5, 6):
            self.c[k].wait_recv()


class RingSum:
    def __init__(self, links, out, via, got, place, dev_left, dev_right):
        self.out, self.via, self.got = out, via, got
        self.place = place
        self.left, self.right = lax.rem(place + 3, 4), lax.rem(place + 1, 4)
        far = lax.rem(place + 2, 4)
        cp = links.copy
        self.c = [
            cp(out.at[far, 0], via.at[0], dev_right),
            cp(out.at[far, 1], via.at[1], dev_left),
            cp(out.at[self.right, 1], got.at[0, 1], dev_right),
            cp(out.at[self.left, 0], got.at[1, 0], dev_left),
            cp(out.at[self.right, 0], got.at[0, 0], dev_right),
            cp(out.at[self.left, 1], got.at[1, 1], dev_left),
        ]

    def begin(self):
        for k in range(4):
            self.c[k].start()

    def relay(self):
        for k, there in ((0, self.right), (1, self.left)):
            self.c[k].wait_recv()
            both = self.out[there, k].astype(F32) + self.via[k].astype(F32)
            self.out[there, k] = both.astype(BF16)
            self.c[4 + k].start()

    def end(self):
        for k in (2, 3, 4, 5):
            self.c[k].wait_recv()

    def arrived(self, half):
        return self.got[0, half].astype(F32) + self.got[1, half].astype(F32)


class LineSum:
    def __init__(self, links, out, got, place, device_of):
        self.got = got
        self.c = []
        for k in (1, 2, 3):
            there = lax.rem(place + k, 4)
            self.c.append(links.copy(out.at[there], got.at[k - 1], device_of(there)))

    def begin(self):
        for c in self.c:
            c.start()

    def end(self):
        for c in self.c:
            c.wait_recv()

    def arrived(self):
        return self.got[0].astype(F32) + self.got[1].astype(F32) + self.got[2].astype(F32)


def kernel(
    pos_hbm, doc_hbm, x_hbm, q_hbm, k_hbm, v_hbm, og_hbm, out_ref,
    pos_ref, doc_ref, k_all, v_all, q_v, og_v, x_v, xt, g, key_at, bias_at, slot_at,
    part, pair_out, pair_got, keep, sx_out, sx_got,
    y_out, y_via, y_got, z_own, z_out, z_got, f_own, f_out, f_got, early, probs_at,
    local_sems, known_sems, send_sems, recv_sems,
):
    me, dp = lax.axis_index("seq"), lax.axis_index("dp")
    x, c = me // 2, me % 2
    z, y = dp // 4, dp % 4
    zh, zl = z // 4, z % 4

    def at_x(place, core):
        return lax.rem(place, 4) * 2 + core

    left, right, far, pair = at_x(x + 3, c), at_x(x + 1, c), at_x(x + 2, c), at_x(x, 1 - c)
    step = 1 + 2 * c
    next_x, prev_x = x + step, x + 4 - step
    dev_next, dev_pair = (at_x(next_x, c), dp), (pair, dp)
    y_left = (me, z * 4 + lax.rem(y + 3, 4))
    y_right = (me, z * 4 + lax.rem(y + 1, 4))

    def near(place):
        return (me, (zh * 4 + place) * 4 + y)

    def group(place):
        return (me, (lax.rem(place, 8) * 4 + zl) * 4 + y)

    def at_z(shift):
        return (me, lax.rem(z + shift + 32, 32) * 4 + y)

    loads = [
        pltpu.make_async_copy(k_hbm, k_all.at[me], local_sems.at[0]),
        pltpu.make_async_copy(v_hbm, v_all.at[me], local_sems.at[1]),
        pltpu.make_async_copy(x_hbm, x_v, local_sems.at[2]),
        pltpu.make_async_copy(q_hbm, q_v, local_sems.at[3]),
        pltpu.make_async_copy(og_hbm, og_v, local_sems.at[4]),
        pltpu.make_async_copy(pos_hbm, pos_ref, local_sems.at[5]),
        pltpu.make_async_copy(doc_hbm, doc_ref, local_sems.at[6]),
    ]
    for load in loads:
        load.start()

    barrier = pltpu.get_barrier_semaphore()
    peers = [(left, dp), (right, dp), (pair, dp), y_left, y_right, at_z(-1), at_z(1)]
    for peer in peers:
        pl.semaphore_signal(barrier, inc=1, device_id=peer, device_id_type=MESH)
    pl.semaphore_wait(barrier, len(peers))

    links = Links(send_sems, recv_sems)
    ring = (me, pair, at_x(prev_x, c), at_x(prev_x, 1 - c), far, dev_next, dev_pair)
    gather_k = Gather(links, lambda d: k_all.at[d], ring)
    gather_v = Gather(links, lambda d: v_all.at[d], ring)
    loads[0].wait()
    gather_k.begin()
    loads[1].wait()
    gather_v.begin()

    def tell(r):
        for side, way in enumerate((1, -1)):
            pl.semaphore_signal(
                known_sems.at[2 * r + side], inc=1, device_id=at_z(way * 2**r), device_id_type=MESH
            )

    def hear(r):
        for side in range(2):
            pl.semaphore_wait(known_sems.at[2 * r + side], 1)

    tell(0)
    loads[5].wait()
    loads[6].wait()

    hits = []
    for q in range(2):
        mine = pos_ref[0, me * 2 + q]
        doc = doc_ref[0, mine]
        key_at[q * 4] = me * 2 + q
        bias_at[q * 4] = jnp.float32(0.0)
        for j in range(1, 4):
            want = jnp.maximum(mine - j, 0)
            live = jnp.logical_and(mine >= j, doc_ref[0, want] == doc)
            spot = jnp.int32(0)
            for s in range(16):
                spot = jnp.where(pos_ref[0, s] == want, jnp.int32(s), spot)
            key_at[q * 4 + j] = spot
            bias_at[q * 4 + j] = jnp.where(live, jnp.float32(0.0), jnp.float32(FILL))
            hits.append((q, q * 4 + j, jnp.where(live, spot, jnp.int32(-1))))
    for s in range(16):
        for q in range(2):
            slot = jnp.int32(8)
            for owner, number, spot in hits:
                if owner == q:
                    slot = jnp.where(spot == s, jnp.int32(number), slot)
            slot_at[q * 16 + s] = slot

    gather_k.mate()
    gather_v.mate()

    loads[2].wait()
    new = lax.broadcasted_iota(jnp.int32, (512, 512), 0)
    old = lax.broadcasted_iota(jnp.int32, (512, 512), 1)
    source = (new // 4 % 8) * 64 + (new // 32 % 4) * 16 + (new // 128) * 4 + new % 4
    one_hot = (old == source).astype(F32).astype(BF16)

    def flip(t, carry):
        at = pl.multiple_of(t * 256, 256)
        xt[:, pl.ds(at, 256)] = dot(one_hot, x_v[pl.ds(at, 256), :], NT).astype(BF16)
        return carry

    lax.fori_loop(0, 2, flip, 0)
    gather_k.relay()
    gather_v.relay()
    hear(0)
    tell(1)
    lax.fori_loop(2, 5, flip, 0)
    gather_k.share()
    gather_v.share()
    lax.fori_loop(5, 7, flip, 0)
    gather_k.last()
    gather_v.last()
    hear(1)
    tell(2)
    lax.fori_loop(7, 8, flip, 0)
    part[...] = jnp.zeros_like(part)
    loads[3].wait()
    loads[4].wait()
    gather_k.end()

    scaling = HD ** (-0.5)
    key_row = lax.broadcasted_iota(jnp.int32, (BLK, 2 * BLK), 0)
    query_col = lax.broadcasted_iota(jnp.int32, (BLK, 2 * BLK), 1) % BLK
    causal = key_row <= query_col

    def operands(number):
        pair_of_heads, q = number // 2, number % 2
        cols = pl.ds(pl.multiple_of(pair_of_heads * 256, 256), 256)
        return pair_of_heads, q, cols

    def stacked(two):
        return jnp.concatenate([two[:, :HD], two[:, HD:]], axis=0)

    def four_blocks(ref, q):
        spots = [key_at[q * 4 + j] for j in range(4)]
        return jnp.concatenate([ref[spot // 2, spot % 2] for spot in spots], axis=0)

    def weigh_keys(number, carry):
        _, q, cols = operands(number)
        scores = dot(four_blocks(k_all, q), stacked(q_v[q, :, cols]), NT) * scaling
        masked = [jnp.where(causal, scores[:BLK], FILL)]
        for j in range(1, 4):
            masked.append(scores[j * BLK : (j + 1) * BLK] + bias_at[q * 4 + j])
        scores = jnp.concatenate(masked, axis=0)
        peak = jnp.max(scores, axis=0, keepdims=True)
        weights = jnp.exp(scores - peak)
        probs_at[number] = weights * (1.0 / jnp.sum(weights, axis=0, keepdims=True))
        return carry

    def attend(number, carry):
        pair_of_heads, q, cols = operands(number)
        queries, grads = stacked(q_v[q, :, cols]), stacked(og_v[q, :, cols])
        keys, values = four_blocks(k_all, q), four_blocks(v_all, q)
        probs = probs_at[number]
        probs_b = probs.astype(BF16)
        dprobs = dot(values, grads, NT)
        delta = jnp.sum(probs_b.astype(F32) * dprobs, axis=0, keepdims=True)
        dscores = (probs * (dprobs - delta)).astype(BF16)
        dq = (dot(dscores, keys, TN) * scaling).astype(BF16)
        g[pair_of_heads, me, q] = jnp.concatenate([dq[:BLK], dq[BLK:]], axis=1)
        dk = dot(dscores, queries, NN) * scaling
        dv = dot(probs_b, grads, NN)
        for j in range(4):
            block = slice(j * BLK, (j + 1) * BLK)
            part[q * 4 + j, :, :HD] += dk[block]
            part[q * 4 + j, :, HD:] += dv[block]
        return carry

    gather_a, gather_b = (Gather(links, lambda d, n=n: g.at[n, d], ring) for n in range(2))
    gather_c = [Gather(links, lambda d, h=h: g.at[2, d, h], ring) for h in range(2)]
    lax.fori_loop(0, 4, weigh_keys, 0, unroll=2)
    gather_v.end()
    lax.fori_loop(0, 2, attend, 0, unroll=True)
    gather_a.begin()
    lax.fori_loop(2, 4, attend, 0, unroll=True)
    gather_a.mate()

    def roles(core):
        ahead = x + 1 + 2 * core
        return at_x(x + 2, core), at_x(ahead, 1 - core), at_x(ahead, core), at_x(x, core)

    def to_block(device, half):
        s = device * 2 + half
        return part[slot_at[s]] + part[slot_at[16 + s]]

    for r, device in enumerate(roles(1 - c)):
        for half in range(2):
            pair_out[r, half] = to_block(device, half).astype(BF16)
    pair_copy = links.copy(pair_out, pair_got, dev_pair)
    pair_copy.start()
    for r, device in enumerate(roles(c)):
        for half in range(2):
            keep[r, half] = to_block(device, half)
    sum_far = links.copy(sx_out.at[0], sx_got.at[0], dev_next)
    sum_other = links.copy(sx_out.at[1], sx_got.at[1], dev_next)
    sum_same = links.copy(sx_out.at[2], sx_got.at[2], dev_next)
    sum_cross = links.copy(sx_got.at[1], sx_got.at[3], dev_pair)
    pair_copy.wait_recv()
    for r in range(4):
        for half in range(2):
            total = keep[r, half] + pair_got[r, half].astype(F32)
            if r < 2:
                sx_out[r, half] = total.astype(BF16)
            else:
                keep[r, half] = total
        if r == 0:
            sum_far.start()
        if r == 1:
            sum_other.start()
    hear(2)
    tell(3)
    gather_a.relay()
    sum_far.wait_recv()
    for half in range(2):
        sx_out[2, half] = (keep[2, half] + sx_got[0, half].astype(F32)).astype(BF16)
    sum_same.start()
    gather_b.begin()
    gather_a.share()
    sum_other.wait_recv()
    sum_cross.start()
    gather_b.mate()
    sum_same.wait_recv()
    sum_cross.wait_recv()
    for half in range(2):
        moved = sx_got[2, half].astype(F32) + sx_got[3, half].astype(F32)
        g[2, me, half] = (part[half * 4] + keep[3, half] + moved).astype(BF16)
    for some in gather_c:
        some.begin()
    gather_a.last()

    def product(n, devices):
        total = None
        for device in devices:
            tokens = pl.ds(pl.multiple_of(device * 256, 256), 256)
            term = dot(xt[:, tokens], g[n, device].reshape(256, 256), NN)
            total = term if total is None else total + term
        return total

    def weigh(n, term=None):
        if term is None:
            term = dot(xt[...], g[n].reshape(2048, 256), NN)
        term = term.astype(BF16)
        for k in range(4):
            for half in range(2):
                at = k * 128 + half * 64
                y_out[n, k, half] = term[at : at + 64]
        sums = RingSum(links, y_out.at[n], y_via.at[n], y_got.at[n], y, y_left, y_right)
        sums.begin()
        return sums

    def to_line(n, sums):
        sums.end()
        for half in range(2):
            total = y_out[n, y, half].astype(F32) + sums.arrived(half)
            for k in range(2):
                some = total[k * 32 : (k + 1) * 32]
                z_own[n, half * 2 + k] = some
                z_out[n, half * 2 + k] = some.astype(BF16)
        line = LineSum(links, z_out.at[n], z_got.at[n], zl, near)
        line.begin()
        return line

    order = (4, 3, 5, 2, 6, 1, 7)

    def to_far(n, line):
        line.end()
        total = z_own[n, zl] + line.arrived()
        for k in range(8):
            some = total[k * 4 : (k + 1) * 4]
            f_own[n, k] = some
            f_out[n, k] = some.astype(BF16)
        sends = []
        for i, shift in enumerate(order):
            there = lax.rem(zh + shift, 8)
            sends.append(links.copy(f_out.at[n, there], f_got.at[n, i], group(there)))
            sends[-1].start()
        return sends

    for some in gather_c:
        some.mate()
    gather_b.relay()
    gather_a.end()
    sum_a = weigh(0)
    for some in gather_c:
        some.relay()
    gather_b.share()
    for some in gather_c:
        some.share()
    gather_b.last()
    sum_a.relay()
    early[...] = product(2, (me, pair, at_x(prev_x, c), at_x(prev_x, 1 - c)))
    for some in gather_c:
        some.last()
    gather_b.end()
    sum_b = weigh(1)
    for some in gather_c:
        some.end()
    sum_c = weigh(2, early[...] + product(2, (at_x(next_x, c), at_x(next_x, 1 - c), far, at_x(x + 2, 1 - c))))
    sum_b.relay()
    sum_c.relay()
    line_a = to_line(0, sum_a)
    line_b = to_line(1, sum_b)
    line_c = to_line(2, sum_c)
    hear(3)
    far_a = to_far(0, line_a)
    far_b = to_far(1, line_b)
    far_c = to_far(2, line_c)
    for n, sends in enumerate((far_a, far_b, far_c)):
        total = f_own[n, zh]
        for i in reversed(range(7)):
            sends[i].wait_recv()
            total = total + f_got[n, i].astype(F32)
        out_ref[:, n * 256 : (n + 1) * 256] = total
    for made in links.sent:
        made.wait_send()
    assert links.count == COPIES


def body(layer_input, query_proj, key_proj, value_proj, out_grad, block_pos, doc_ids):
    hbm = pl.BlockSpec(memory_space=pl.ANY)

    return pl.pallas_call(
        kernel,
        out_shape=jax.ShapeDtypeStruct((4, 768), F32),
        in_specs=[hbm, hbm, hbm, hbm, hbm, hbm, hbm],
        out_specs=pl.BlockSpec(memory_space=pltpu.VMEM),
        scratch_shapes=[
            pltpu.SMEM((1, 16), jnp.int32),
            pltpu.SMEM((1, 16), jnp.int32),
            pltpu.VMEM((8, 2, BLK, HD), BF16),
            pltpu.VMEM((8, 2, BLK, HD), BF16),
            pltpu.VMEM((2, BLK, 512), BF16),
            pltpu.VMEM((2, BLK, 512), BF16),
            pltpu.VMEM((2048, 512), BF16),
            pltpu.VMEM((512, 2048), BF16),
            pltpu.VMEM((CHUNKS, 8, 2, BLK, 256), BF16),
            pltpu.SMEM((8,), jnp.int32),
            pltpu.SMEM((8,), F32),
            pltpu.SMEM((32,), jnp.int32),
            pltpu.VMEM((9, BLK, 256), F32),
            pltpu.VMEM((4, 2, BLK, 256), BF16),
            pltpu.VMEM((4, 2, BLK, 256), BF16),
            pltpu.VMEM((4, 2, BLK, 256), F32),
            pltpu.VMEM((3, 2, BLK, 256), BF16),
            pltpu.VMEM((4, 2, BLK, 256), BF16),
            pltpu.VMEM((CHUNKS, 4, 2, 64, 256), BF16),
            pltpu.VMEM((CHUNKS, 2, 64, 256), BF16),
            pltpu.VMEM((CHUNKS, 2, 2, 64, 256), BF16),
            pltpu.VMEM((CHUNKS, 4, 32, 256), F32),
            pltpu.VMEM((CHUNKS, 4, 32, 256), BF16),
            pltpu.VMEM((CHUNKS, 3, 32, 256), BF16),
            pltpu.VMEM((CHUNKS, 8, 4, 256), F32),
            pltpu.VMEM((CHUNKS, 8, 4, 256), BF16),
            pltpu.VMEM((CHUNKS, 7, 4, 256), BF16),
            pltpu.VMEM((512, 256), F32),
            pltpu.VMEM((4, 512, 256), F32),
            pltpu.SemaphoreType.DMA((7,)),
            pltpu.SemaphoreType.REGULAR((8,)),
            pltpu.SemaphoreType.DMA((COPIES,)),
            pltpu.SemaphoreType.DMA((COPIES,)),
        ],
        compiler_params=pltpu.CompilerParams(
            collective_id=0, has_side_effects=True, vmem_limit_bytes=56 * 1024 * 1024
        ),
    )(
        block_pos,
        doc_ids,
        layer_input.reshape(2048, 512),
        query_proj.reshape(2, BLK, 512),
        key_proj.reshape(2, BLK, HD),
        value_proj.reshape(2, BLK, HD),
        out_grad.reshape(2, BLK, 512),
    )


def solution(mesh):
    placed = (
        P("dp", None, "seq"),
        P("dp", "seq", None),
        P("dp", "seq", None),
        P("dp", "seq", None),
        P("dp", "seq", None),
        P("dp", None),
        P("dp", None),
    )
    return jax.shard_map(
        body, mesh=mesh, in_specs=placed, out_specs=P(("seq", "dp"), None), check_vma=False
    )
```
